512 devices in a mesh: row: 16 (over x_lo, y, core), col: 32 (over x_hi, z).
Axes of the slice: x: 4 (x_hi: 2, x_lo: 2; x = x_hi * 2 + x_lo), y: 4, z: 16, core: 2. Of those that a mesh axis runs over, the one named last changes fastest.
Arguments:
- trailing: bfloat16 [16384, 16384], P('row', 'col'), may hold values from -6 to 6
- left_outer: bfloat16 [1536, 16384], P('col', 'row'), may hold values from -0.625 to 0.625
- left_inner: bfloat16 [1536, 16384], P('col', 'row'), may hold values from -0.1875 to 0.1875
- upper_outer: bfloat16 [1536, 16384], P('row', 'col'), may hold values from -6 to 6
- upper_inner: bfloat16 [1536, 16384], P('row', 'col'), may hold values from -0.15625 to 0.15625
- left_ranks: int32 [16, 16], replicated, may hold values from 16 to 96
- upper_ranks: int32 [16, 16], replicated, may hold values from 16 to 96
Outputs:
- updated: bfloat16 [16384, 16384], P('row', 'col')
- next_panel: bfloat16 [16384, 1024], P(('row', 'col'))
The draws below stay inside these ranges and needn't reach their ends.
All inputs are finite; a program needn't handle non-finite values.
Results may differ from the reference program's by a relative error of at most 0.0042.
Values may be sent and summed in bfloat16 or wider, within the bound.
No kernel may reach another device: no remote copies, remote signals or barrier semaphores. Data moves between devices by JAX's collectives and lax.ppermute only.
A program may use at most 64 MiB of HBM per device.

```python
import jax
import jax.numpy as jnp
from jax import lax

B = 1024
R = 96
NT = 16
ORDER = 16384
N_ROW = 16


def set_ends(drawn, rng, smallest, high):
    longest = drawn.shape.index(max(drawn.shape))
    spots = []
    for shift in (0, 1):
        where = [jax.random.randint(jax.random.fold_in(rng, axis), (), 0, length) for axis, length in enumerate(drawn.shape)]
        where[longest] = (where[longest] + shift) % drawn.shape[longest]
        spots.append(tuple(where))
    return drawn.at[spots[0]].set(smallest).at[spots[1]].set(high)


def levels(stream_key, extent, cuts, smallest, high):
    loudness, own = 1.0, jax.random.fold_in(stream_key, 6)
    for dim, shards_of in cuts:
        steps = jnp.exp(jax.random.uniform(jax.random.fold_in(own, dim), (shards_of,), jnp.float32, smallest / len(cuts), high / len(cuts)))
        loudness = loudness * jnp.repeat(steps, extent[dim] // shards_of).reshape([-1 if axis == dim else 1 for axis in range(len(extent))])
    return loudness


def noise(rng, shape, scale, reach, split=(), kind=jnp.bfloat16):
    result = scale * jax.random.normal(rng, shape, jnp.float32)
    if split:
        result = result * levels(rng, shape, split, -0.22, 0.18)
    return jnp.clip(result, -reach, reach).astype(kind)


def setup_inputs(seed: int = 0) -> dict:
    seeds = jax.random.split(jax.random.key(seed), 8)
    trailing = noise(seeds[0], (ORDER, ORDER), 1.0, 6.0, ((0, 16), (1, 32)))
    left_outer = noise(seeds[1], (NT * R, ORDER), R ** -0.5, 0.625, ((0, 32), (1, 16)))
    left_inner = noise(seeds[2], (NT * R, ORDER), B ** -0.5, 0.1875, ((0, 32), (1, 16)))
    upper_outer = noise(seeds[3], (NT * R, ORDER), 1.0, 6.0, ((0, 16), (1, 32)))
    upper_inner = noise(seeds[4], (NT * R, ORDER), (NT * R) ** -0.5, 0.15625, ((0, 16), (1, 32)))
    left_ranks = set_ends(jax.random.randint(seeds[5], (NT, NT), R // 6, R + 1), jax.random.fold_in(seeds[5], 1), R // 6, R).astype(jnp.int32)
    upper_ranks = set_ends(jax.random.randint(seeds[6], (NT, NT), R // 6, R + 1), jax.random.fold_in(seeds[6], 1), R // 6, R).astype(jnp.int32)
    return dict(trailing=trailing, left_outer=left_outer, left_inner=left_inner, upper_outer=upper_outer, upper_inner=upper_inner, left_ranks=left_ranks, upper_ranks=upper_ranks)


def reference(trailing, left_outer, left_inner, upper_outer, upper_inner, left_ranks, upper_ranks):
    tile_count = N_ROW
    rank_index = jnp.arange(R, dtype=jnp.int32)

    def tile_row(row_tile):
        outer_rows = lax.dynamic_slice_in_dim(left_outer, row_tile * B, B, 1).reshape(tile_count, R, B).astype(jnp.float32)
        interior_rows = lax.dynamic_slice_in_dim(left_inner, row_tile * B, B, 1).reshape(tile_count, R, B).astype(jnp.float32)
        row_ranks = lax.dynamic_index_in_dim(left_ranks, row_tile, 0, keepdims=False)
        left_live = (rank_index[None, :] < row_ranks[:, None]).astype(jnp.float32)

        def tile_col(col_tile):
            top_rows = lax.dynamic_slice_in_dim(upper_outer, col_tile * B, B, 1).reshape(tile_count, R, B).astype(jnp.float32)
            upper_cols = lax.dynamic_slice_in_dim(upper_inner, col_tile * B, B, 1)
            col_ranks = lax.dynamic_index_in_dim(upper_ranks, col_tile, 1, keepdims=False)
            upper_live = (rank_index[None, :] < col_ranks[:, None]).astype(jnp.float32)
            central_block = jnp.einsum("rao,rho->rah", interior_rows, top_rows)
            central_block = (central_block * left_live[:, :, None] * upper_live[:, None, :]).astype(jnp.bfloat16)
            outer_sum = jnp.einsum("ktp,ktu->pku", outer_rows, central_block.astype(jnp.float32))
            outer_sum = outer_sum.reshape(B, tile_count * R).astype(jnp.bfloat16)
            product = jnp.dot(outer_sum, upper_cols, preferred_element_type=jnp.float32)
            dense_block = lax.dynamic_slice(trailing, (row_tile * B, col_tile * B), (B, B)).astype(jnp.float32)
            return (dense_block - product).astype(jnp.bfloat16)

        row_tiles = lax.map(tile_col, jnp.arange(tile_count, dtype=jnp.int32))
        return jnp.transpose(row_tiles, (1, 0, 2)).reshape(B, tile_count * B)

    updated = lax.map(tile_row, jnp.arange(tile_count, dtype=jnp.int32)).reshape(tile_count * B, tile_count * B)
    next_panel = updated[:, 0:B]
    return (updated, next_panel)
```

```python
import jax
import jax.numpy as jnp
from jax import lax
from jax.sharding import Mesh, PartitionSpec as P

R = 96
H = 48
NT = 16
COL = ("xhi", "z")
BF = jnp.bfloat16


def place(branches, default):
    for hit, value in branches:
        default = jnp.where(hit, value, default)
    return default


def spread(updated, col_at):
    sent = []
    for base in (24, 16, 8):
        sent.append(
            (col_at // 8 == base // 8, lax.ppermute(updated[base * 32 : base * 32 + 256], COL, [(0, base), (1, base + 1)]))
        )
    held = place(sent, updated[:256])
    sent = []
    for step in (6, 4, 2):
        pairs = [(b + h, b + step + h) for b in (0, 8, 16, 24) for h in (0, 1)]
        sent.append((col_at % 8 // 2 == step // 2, lax.ppermute(held[step * 32 : step * 32 + 64], COL, pairs)))
    held = place(sent, held[:64])
    odd = col_at % 2 == 1
    kept = jnp.where(odd, held[32:], held[:32])
    given = jnp.where(odd, held[:32], held[32:])
    got = lax.ppermute(given, "z", [(i, i ^ 1) for i in range(16)])
    return jnp.concatenate([jnp.where(odd, got, kept), jnp.where(odd, kept, got)], axis=1)


def body(trailing, left_outer, left_inner, upper_outer, upper_inner, left_ranks, upper_ranks):
    row_at = lax.axis_index("row")
    x_at, z_at = lax.axis_index("xhi"), lax.axis_index("z")
    col_at = x_at * 16 + z_at
    own_tile = col_at // 2

    mine = jnp.stack([left_outer, left_inner])
    other = lax.ppermute(mine, "xhi", [(0, 1), (1, 0)])
    first = x_at == 0
    pair = jnp.stack([jnp.where(first, mine, other), jnp.where(first, other, mine)], axis=1)
    columns = lax.all_gather(pair.reshape(4 * H, -1), "z", axis=0, tiled=True)
    columns = columns.reshape(NT, 2, 2, H, -1)

    partner = lax.ppermute(upper_outer, "z", [(i, i ^ 1) for i in range(16)])
    even = z_at % 2 == 0
    rows = jnp.concatenate(
        [jnp.where(even, upper_outer, partner), jnp.where(even, partner, upper_outer), upper_inner], axis=1
    )
    rows = jnp.broadcast_to(rows[None], (NT,) + rows.shape)
    rows = lax.all_to_all(rows, "row", 0, 0)
    width = trailing.shape[1]
    p_rows = rows[:, :, : 2 * width].reshape(2, 8, R, 2 * width)
    q_rows = rows[:, :, 2 * width :].reshape(2, 8, R, width)

    col_ranks = lax.dynamic_index_in_dim(upper_ranks, own_tile, 1, keepdims=False).reshape(2, 8)
    row_ranks = lax.dynamic_index_in_dim(left_ranks, row_at, 0, keepdims=False).reshape(2, 8)
    rank = jnp.arange(R, dtype=jnp.int32)
    live = (rank.reshape(2, H) < row_ranks[:, :, None, None])[..., None] & (rank < col_ranks[:, :, None])[:, :, None, None, :]

    inner = columns[:, 1].reshape(8, 2, 2, H, -1)
    core = jnp.einsum("zhxrq,xzuq->xzhru", inner, p_rows, preferred_element_type=jnp.float32)
    core = jnp.where(live, core, 0.0).astype(BF)
    weights = jnp.einsum("xzhru,xzup->zhxrp", core, q_rows, preferred_element_type=jnp.float32).astype(BF)
    product = lax.dot_general(
        columns[:, 0].reshape(NT * R, -1),
        weights.reshape(NT * R, width),
        (((0,), (0,)), ((), ())),
        preferred_element_type=jnp.float32,
    )
    updated = (trailing.astype(jnp.float32) - product).astype(BF)
    return updated, spread(updated, col_at)


def solution(mesh):
    fine = Mesh(mesh.devices.reshape(16, 2, 16), ("row", "xhi", "z"))
    grid = P("row", COL)
    turned = P(COL, "row")
    return jax.shard_map(
        body,
        mesh=fine,
        in_specs=(grid, turned, turned, grid, grid, P(), P()),
        out_specs=(grid, P(("row",) + COL, None)),
        check_vma=False,
    )
```

```python
import jax
import jax.numpy as jnp
from jax import lax
from jax.sharding import Mesh, PartitionSpec as P

NT = 16
COL = ("xhi", "z")
TURNED_COL = ("z", "xhi")
BF = jnp.bfloat16
SWAP_Z = [(i, i ^ 1) for i in range(16)]


def place(branches, default):
    for hit, value in branches:
        default = jnp.where(hit, value, default)
    return default


def spread(updated, col_at):
    share = updated.shape[0] // 32
    part = 4 * share
    sent = []
    for m in range(7, 0, -1):
        block = lax.ppermute(updated[m * part : (m + 1) * part], COL, [(0, 4 * m), (1, 4 * m + 1)])
        sent.append((col_at // 4 == m, block))
    held = place(sent, updated[:part])
    spot = col_at % 4
    got = []
    for d in (1, 2, 3):
        piece = lax.dynamic_slice_in_dim(held, (spot + d) % 4 * share, share, 0)
        pairs = [(b + h, b + (h + d) % 4) for b in range(0, 32, 4) for h in (0, 1)]
        got.append(lax.ppermute(piece, COL, pairs))
    own = lax.dynamic_slice_in_dim(held, spot * share, share, 0)
    left = place([(spot == d, got[d - 1]) for d in (1, 2, 3)], own)
    right = place([((spot - 1) % 4 == d, got[d - 1]) for d in (1, 2, 3)], own)
    return jnp.concatenate([left, right], axis=1)


def turn(block, flip):
    pairs = [
        (k * 32 + 2 * j + h, j * 32 + 2 * k + (h ^ flip)) for k in range(NT) for j in range(NT) for h in (0, 1)
    ]
    return lax.ppermute(block, ("row",) + COL, pairs)


def body(trailing, left_outer, left_inner, upper_outer, upper_inner, left_ranks, upper_ranks):
    row_at = lax.axis_index("row")
    x_at, z_at = lax.axis_index("xhi"), lax.axis_index("z")
    col_at = x_at * 16 + z_at
    pair_at = col_at // 2
    even = z_at % 2 == 0
    width = trailing.shape[1]
    rank_pad, half = upper_outer.shape[0], left_outer.shape[0]

    other = lax.ppermute(left_outer, "xhi", [(0, 1), (1, 0)])
    first = x_at == 0
    outer = jnp.concatenate([jnp.where(first, left_outer, other), jnp.where(first, other, left_outer)], axis=0)
    outer = lax.all_gather(outer, "z", axis=0, tiled=True)

    same, crossed = turn(upper_outer, 0), turn(upper_outer, 1)
    p_block = jnp.concatenate([jnp.where(even, same, crossed), jnp.where(even, crossed, same)], axis=1)
    p_all = lax.all_to_all(jnp.broadcast_to(p_block[None], (NT,) + p_block.shape), "row", 0, 0)
    q_all = lax.all_to_all(jnp.broadcast_to(upper_inner[None], (NT,) + upper_inner.shape), "row", 0, 0)

    core = jnp.einsum("tq,juq->jtu", left_inner, p_all, preferred_element_type=jnp.float32)
    rank = jnp.arange(rank_pad, dtype=jnp.int32)
    t_at = (col_at % 2) * half + jnp.arange(half, dtype=jnp.int32)
    t_live = t_at < lax.dynamic_slice(left_ranks, (row_at, pair_at), (1, 1))[0]
    u_live = rank[None, :] < lax.dynamic_index_in_dim(upper_ranks, pair_at, 0, keepdims=False)[:, None]
    core = jnp.where(t_live[None, :, None] & u_live[:, None, :], core, 0.0).astype(BF)
    core = core.reshape(2, 8, 1, half, rank_pad).transpose(1, 2, 0, 3, 4)
    core = jnp.broadcast_to(core, (8, 2, 2, half, rank_pad)).reshape(32, half, rank_pad)
    core = lax.all_to_all(core, TURNED_COL, 0, 0)

    weights = jnp.einsum(
        "zhxru,xzup->zhxrp",
        core.reshape(8, 2, 2, half, rank_pad),
        q_all.reshape(2, 8, rank_pad, width),
        preferred_element_type=jnp.float32,
    ).astype(BF)
    product = lax.dot_general(
        outer, weights.reshape(NT * rank_pad, width), (((0,), (0,)), ((), ())), preferred_element_type=jnp.float32
    )
    updated = (trailing.astype(jnp.float32) - product).astype(BF)
    return updated, spread(updated, col_at)


def solution(mesh):
    fine = Mesh(mesh.devices.reshape(16, 2, 16), ("row", "xhi", "z"))
    grid = P("row", COL)
    turned = P(COL, "row")
    return jax.shard_map(
        body,
        mesh=fine,
        in_specs=(grid, turned, turned, grid, grid, P(), P()),
        out_specs=(grid, P(("row",) + COL, None)),
        check_vma=False,
    )
```

```python
import jax
import jax.numpy as jnp
from jax import lax
from jax.experimental import pallas as pl
from jax.experimental.pallas import tpu as pltpu
from jax.sharding import Mesh, PartitionSpec as P

NT = 16
COL = ("xhi", "z")
BF = jnp.bfloat16
SWAP_Z = [(i, i ^ 1) for i in range(16)]
STEP = 2


def place(branches, default):
    for hit, value in branches:
        default = jnp.where(hit, value, default)
    return default


def spread(updated, col_at):
    share = updated.shape[0] // 32
    part = 4 * share
    sent = []
    for m in range(7, 0, -1):
        block = lax.ppermute(updated[m * part : (m + 1) * part], COL, [(0, 4 * m), (1, 4 * m + 1)])
        sent.append((col_at // 4 == m, block))
    held = place(sent, updated[:part])
    spot = col_at % 4
    got = []
    for d in (1, 2, 3):
        piece = lax.dynamic_slice_in_dim(held, (spot + d) % 4 * share, share, 0)
        pairs = [(b + h, b + (h + d) % 4) for b in range(0, 32, 4) for h in (0, 1)]
        got.append(lax.ppermute(piece, COL, pairs))
    own = lax.dynamic_slice_in_dim(held, spot * share, share, 0)
    left = place([(spot == d, got[d - 1]) for d in (1, 2, 3)], own)
    right = place([((spot - 1) % 4 == d, got[d - 1]) for d in (1, 2, 3)], own)
    return jnp.concatenate([left, right], axis=1)


def update_kernel(x_at_ref, left_ref, upper_ref, cols_ref, rows_ref, trailing_ref, out_ref, acc_ref):
    step = pl.program_id(0)
    rank_pad = rows_ref.shape[2]
    depth = cols_ref.shape[4]
    t = lax.broadcasted_iota(jnp.int32, (rank_pad, rank_pad), 0)
    u = lax.broadcasted_iota(jnp.int32, (rank_pad, rank_pad), 1)
    outers, weights = [], []
    for local in range(STEP):
        for slot in range(2):
            xhi = slot ^ x_at_ref[0]
            k = xhi * 8 + step * STEP + local
            inner = jnp.concatenate([cols_ref[2 * local, slot, 1], cols_ref[2 * local + 1, slot, 1]], axis=0)
            core = lax.dot_general(
                inner,
                rows_ref[xhi, local, :, :depth],
                (((1,), (1,)), ((), ())),
                preferred_element_type=jnp.float32,
            )
            core = jnp.where((t < left_ref[k]) & (u < upper_ref[k]), core, 0.0).astype(BF)
            weights.append(
                jnp.dot(core, rows_ref[xhi, local, :, depth:], preferred_element_type=jnp.float32).astype(BF)
            )
            outers += [cols_ref[2 * local, slot, 0], cols_ref[2 * local + 1, slot, 0]]
    product = lax.dot_general(
        jnp.concatenate(outers, axis=0),
        jnp.concatenate(weights, axis=0),
        (((0,), (0,)), ((), ())),
        preferred_element_type=jnp.float32,
    )

    @pl.when(step == 0)
    def _():
        acc_ref[...] = product

    @pl.when(step > 0)
    def _():
        acc_ref[...] += product

    @pl.when(step == pl.num_programs(0) - 1)
    def _():
        out_ref[...] = (trailing_ref[...].astype(jnp.float32) - acc_ref[...]).astype(BF)


def update(x_at, left, upper, cols, rows, trailing):
    height, width = trailing.shape
    rank_pad, depth = rows.shape[2], cols.shape[4]
    half = cols.shape[3]
    return pl.pallas_call(
        update_kernel,
        out_shape=jax.ShapeDtypeStruct(trailing.shape, BF),
        grid_spec=pltpu.PrefetchScalarGridSpec(
            num_scalar_prefetch=3,
            grid=(8 // STEP,),
            in_specs=[
                pl.BlockSpec((2 * STEP, 2, 2, half, depth), lambda i, *_: (i, 0, 0, 0, 0)),
                pl.BlockSpec((2, STEP, rank_pad, depth + width), lambda i, *_: (0, i, 0, 0)),
                pl.BlockSpec((height, width), lambda i, *_: (0, 0)),
            ],
            out_specs=pl.BlockSpec((height, width), lambda i, *_: (0, 0)),
            scratch_shapes=[pltpu.VMEM((height, width), jnp.float32)],
        ),
        compiler_params=pltpu.CompilerParams(dimension_semantics=("arbitrary",), vmem_limit_bytes=40 << 20),
    )(x_at, left, upper, cols, rows, trailing)


def body(trailing, left_outer, left_inner, upper_outer, upper_inner, left_ranks, upper_ranks):
    row_at = lax.axis_index("row")
    x_at, z_at = lax.axis_index("xhi"), lax.axis_index("z")
    col_at = x_at * 16 + z_at
    half = left_outer.shape[0]

    mine = jnp.concatenate([left_outer, left_inner], axis=0)
    other = lax.ppermute(mine, "xhi", [(0, 1), (1, 0)])
    cols = lax.all_gather(jnp.concatenate([mine, other], axis=0), "z", axis=0, tiled=True)
    cols = cols.reshape(NT, 2, 2, half, -1)

    partner = lax.ppermute(upper_outer, "z", SWAP_Z)
    even = z_at % 2 == 0
    rows = jnp.concatenate(
        [jnp.where(even, upper_outer, partner), jnp.where(even, partner, upper_outer), upper_inner], axis=1
    )
    rows = lax.all_to_all(jnp.broadcast_to(rows[None], (NT,) + rows.shape), "row", 0, 0)
    rows = rows.reshape((2, 8) + rows.shape[1:])

    left = lax.dynamic_index_in_dim(left_ranks, row_at, 0, keepdims=False)
    upper = lax.dynamic_index_in_dim(upper_ranks, col_at // 2, 1, keepdims=False)
    updated = update(x_at.reshape(1).astype(jnp.int32), left, upper, cols, rows, trailing)
    return updated, spread(updated, col_at)


def solution(mesh):
    fine = Mesh(mesh.devices.reshape(16, 2, 16), ("row", "xhi", "z"))
    grid = P("row", COL)
    turned = P(COL, "row")
    return jax.shard_map(
        body,
        mesh=fine,
        in_specs=(grid, turned, turned, grid, grid, P(), P()),
        out_specs=(grid, P(("row",) + COL, None)),
        check_vma=False,
    )
```

```python
import jax
import jax.numpy as jnp
from jax import lax
from jax.experimental import pallas as pl
from jax.experimental.pallas import tpu as pltpu
from jax.sharding import Mesh, PartitionSpec as P

NT = 16
COL = ("xhi", "z")
BF = jnp.bfloat16
SWAP_Z = [(i, i ^ 1) for i in range(16)]
LIMIT = 28


def place(branches, default):
    for hit, value in branches:
        default = jnp.where(hit, value, default)
    return default


def spread(updated, parts, col_at):
    share = updated.shape[0] // 32
    part = 4 * share
    sent = []
    for m in range(7, 0, -1):
        block = lax.ppermute(parts[m - 1], COL, [(0, 4 * m), (1, 4 * m + 1)])
        sent.append((col_at // 4 == m, block))
    held = place(sent, updated[:part])
    spot = col_at % 4
    got = []
    for d in (1, 2, 3):
        piece = lax.dynamic_slice_in_dim(held, (spot + d) % 4 * share, share, 0)
        pairs = [(b + h, b + (h + d) % 4) for b in range(0, 32, 4) for h in (0, 1)]
        got.append(lax.ppermute(piece, COL, pairs))
    own = lax.dynamic_slice_in_dim(held, spot * share, share, 0)
    left = place([(spot == d, got[d - 1]) for d in (1, 2, 3)], own)
    right = place([((spot - 1) % 4 == d, got[d - 1]) for d in (1, 2, 3)], own)
    return jnp.concatenate([left, right], axis=1)


def update_kernel(
    x_at_ref, left_ref, upper_ref, cols_ref, p_ref, q_ref, trailing_ref, out_ref, *rest
):
    parts, (outer_ref, inner_ref, weights_ref, q_held, dense_ref, sems) = rest[:7], rest[7:]
    rank_pad = p_ref.shape[2]
    depth = cols_ref.shape[4]
    copies = []

    def fetch(source, target):
        copies.append(pltpu.make_async_copy(source, target, sems.at[len(copies)]))

    for zz in range(8):
        for h in range(2):
            fetch(cols_ref.at[2 * zz + h, :, 1], inner_ref.at[zz, :, h])
        fetch(q_ref.at[:, zz], q_held.at[:, zz])
    for zz in range(8):
        for h in range(2):
            fetch(cols_ref.at[2 * zz + h, :, 0], outer_ref.at[zz, :, h])
    fetch(trailing_ref, dense_ref)
    for copy in copies:
        copy.start()
    t = lax.broadcasted_iota(jnp.int32, (rank_pad, rank_pad), 0)
    u = lax.broadcasted_iota(jnp.int32, (rank_pad, rank_pad), 1)
    for zz in range(8):
        for copy in copies[3 * zz : 3 * zz + 3]:
            copy.wait()
        for slot in range(2):
            xhi = slot ^ x_at_ref[0]
            k = xhi * 8 + zz
            core = lax.dot_general(
                inner_ref[zz, slot].reshape(rank_pad, depth),
                p_ref[xhi, zz],
                (((1,), (1,)), ((), ())),
                preferred_element_type=jnp.float32,
            )
            core = jnp.where((t < left_ref[k]) & (u < upper_ref[k]), core, 0.0).astype(BF)
            at = (2 * zz + slot) * rank_pad
            weights_ref[at : at + rank_pad, :] = jnp.dot(
                core, q_held[xhi, zz], preferred_element_type=jnp.float32
            ).astype(BF)
    for copy in copies[24:]:
        copy.wait()
    outer = outer_ref[...].reshape(NT * rank_pad, depth)
    product = lax.dot_general(outer, weights_ref[...], (((0,), (0,)), ((), ())), preferred_element_type=jnp.float32)
    done = (dense_ref[...].astype(jnp.float32) - product).astype(BF)
    out_ref[...] = done
    part = done.shape[0] // 8
    for m in range(1, 8):
        parts[m - 1][...] = done[m * part : (m + 1) * part]


def update(x_at, left, upper, cols, p_rows, q_rows, trailing):
    height, width = trailing.shape
    rank_pad, depth, half = p_rows.shape[2], cols.shape[4], cols.shape[3]
    vmem, smem = pl.BlockSpec(memory_space=pltpu.VMEM), pl.BlockSpec(memory_space=pltpu.SMEM)
    hbm = pl.BlockSpec(memory_space=pltpu.HBM)
    held = pltpu.VMEM((8, 2, 2, half, depth), BF)
    return pl.pallas_call(
        update_kernel,
        out_shape=[jax.ShapeDtypeStruct((height, width), BF)] + [jax.ShapeDtypeStruct((height // 8, width), BF)] * 7,
        in_specs=[smem, smem, smem, hbm, vmem, hbm, hbm],
        out_specs=[vmem] * 8,
        scratch_shapes=[held, held, pltpu.VMEM((NT * rank_pad, width), BF), pltpu.VMEM(q_rows.shape, BF), pltpu.VMEM(trailing.shape, BF), pltpu.SemaphoreType.DMA((41,))],
        compiler_params=pltpu.CompilerParams(vmem_limit_bytes=LIMIT << 20),
    )(
        x_at,
        left,
        upper,
        pltpu.with_memory_space_constraint(cols, pltpu.HBM),
        p_rows,
        pltpu.with_memory_space_constraint(q_rows, pltpu.HBM),
        pltpu.with_memory_space_constraint(trailing, pltpu.HBM),
    )


def body(trailing, left_outer, left_inner, upper_outer, upper_inner, left_ranks, upper_ranks):
    row_at = lax.axis_index("row")
    x_at, z_at = lax.axis_index("xhi"), lax.axis_index("z")
    col_at = x_at * 16 + z_at
    half = left_outer.shape[0]

    mine = jnp.concatenate([left_outer, left_inner], axis=0)
    other = lax.ppermute(mine, "xhi", [(0, 1), (1, 0)])
    cols = lax.all_gather(jnp.concatenate([mine, other], axis=0), "z", axis=0, tiled=True)
    cols = cols.reshape(NT, 2, 2, half, -1)

    partner = lax.ppermute(upper_outer, "z", SWAP_Z)
    even = z_at % 2 == 0
    rows = jnp.concatenate(
        [jnp.where(even, upper_outer, partner), jnp.where(even, partner, upper_outer), upper_inner], axis=1
    )
    rows = lax.all_to_all(jnp.broadcast_to(rows[None], (NT,) + rows.shape), "row", 0, 0)
    rows = rows.reshape((2, 8) + rows.shape[1:])
    depth = cols.shape[-1]
    p_rows, q_rows = rows[..., :depth], rows[..., depth:]

    left = lax.dynamic_index_in_dim(left_ranks, row_at, 0, keepdims=False)
    upper = lax.dynamic_index_in_dim(upper_ranks, col_at // 2, 1, keepdims=False)
    updated, *parts = update(x_at.reshape(1).astype(jnp.int32), left, upper, cols, p_rows, q_rows, trailing)
    return updated, spread(updated, parts, col_at)


def solution(mesh):
    fine = Mesh(mesh.devices.reshape(16, 2, 16), ("row", "xhi", "z"))
    grid = P("row", COL)
    turned = P(COL, "row")
    return jax.shard_map(
        body,
        mesh=fine,
        in_specs=(grid, turned, turned, grid, grid, P(), P()),
        out_specs=(grid, P(("row",) + COL, None)),
        check_vma=False,
    )
```

```python
import jax
import jax.numpy as jnp
from jax import lax
from jax.experimental import pallas as pl
from jax.experimental.pallas import tpu as pltpu
from jax.sharding import Mesh, PartitionSpec as P

NT = 16
ROW = ("chip", "core")
COL = ("xhi", "z")
BF = jnp.bfloat16
SWAP_Z = [(i, i ^ 1) for i in range(16)]
LIMIT = 28


def place(branches, default):
    for hit, value in branches:
        default = jnp.where(hit, value, default)
    return default


def spread(updated, parts, col_at):
    share = updated.shape[0] // 32
    sent = []
    for m in (3, 2, 1):
        block = lax.ppermute(parts[m - 1], COL, [(0, 8 * m), (1, 8 * m + 1)])
        sent.append((col_at // 8 == m, block))
    held = place(sent, updated[: 8 * share])
    spot = col_at % 8
    got = []
    for d in range(1, 8):
        piece = lax.dynamic_slice_in_dim(held, (spot + d) % 8 * share, share, 0)
        pairs = [(b + h, b + (h + d) % 8) for b in range(0, 32, 8) for h in (0, 1)]
        got.append(lax.ppermute(piece, COL, pairs))
    own = lax.dynamic_slice_in_dim(held, spot * share, share, 0)
    left = place([(spot == d, got[d - 1]) for d in range(1, 8)], own)
    right = place([((spot - 1) % 8 == d, got[d - 1]) for d in range(1, 8)], own)
    return jnp.concatenate([left, right], axis=1)


def update_kernel(
    x_at_ref, left_ref, upper_ref, cols_ref, p_ref, q_ref, trailing_ref, out_ref, *rest
):
    parts, (outer_ref, inner_ref, weights_ref, q_held, dense_ref, sems) = rest[:3], rest[3:]
    rank_pad = p_ref.shape[2]
    depth = cols_ref.shape[4]
    copies = []

    def fetch(source, target):
        copies.append(pltpu.make_async_copy(source, target, sems.at[len(copies)]))

    for zz in range(8):
        for h in range(2):
            fetch(cols_ref.at[2 * zz + h, :, 1], inner_ref.at[zz, :, h])
        fetch(q_ref.at[:, zz], q_held.at[:, zz])
    for zz in range(8):
        for h in range(2):
            fetch(cols_ref.at[2 * zz + h, :, 0], outer_ref.at[zz, :, h])
    fetch(trailing_ref, dense_ref)
    for copy in copies[:12]:
        copy.start()
    t = lax.broadcasted_iota(jnp.int32, (rank_pad, rank_pad), 0)
    u = lax.broadcasted_iota(jnp.int32, (rank_pad, rank_pad), 1)
    for zz in range(8):
        for copy in copies[3 * zz : 3 * zz + 3]:
            copy.wait()
        if zz < 4:
            for copy in copies[3 * zz + 12 : 3 * zz + 15]:
                copy.start()
        for copy in copies[2 * zz + 24 : 2 * zz + 26]:
            copy.start()
        if zz == 7:
            copies[40].start()
        for slot in range(2):
            xhi = slot ^ x_at_ref[0]
            k = xhi * 8 + zz
            core = lax.dot_general(
                inner_ref[zz, slot].reshape(rank_pad, depth),
                p_ref[xhi, zz],
                (((1,), (1,)), ((), ())),
                preferred_element_type=jnp.float32,
            )
            core = jnp.where((t < left_ref[k]) & (u < upper_ref[k]), core, 0.0).astype(BF)
            at = (2 * zz + slot) * rank_pad
            weights_ref[at : at + rank_pad, :] = jnp.dot(
                core, q_held[xhi, zz], preferred_element_type=jnp.float32
            ).astype(BF)
    for copy in copies[24:]:
        copy.wait()
    outer = outer_ref[...].reshape(NT * rank_pad, depth)
    product = lax.dot_general(outer, weights_ref[...], (((0,), (0,)), ((), ())), preferred_element_type=jnp.float32)
    done = (dense_ref[...].astype(jnp.float32) - product).astype(BF)
    out_ref[...] = done
    part = done.shape[0] // 4
    for m in range(1, 4):
        parts[m - 1][...] = done[m * part : (m + 1) * part]


def update(x_at, left, upper, cols, p_rows, q_rows, trailing):
    height, width = trailing.shape
    rank_pad, depth, half = p_rows.shape[2], cols.shape[4], cols.shape[3]
    vmem, smem = pl.BlockSpec(memory_space=pltpu.VMEM), pl.BlockSpec(memory_space=pltpu.SMEM)
    hbm = pl.BlockSpec(memory_space=pltpu.HBM)
    held = pltpu.VMEM((8, 2, 2, half, depth), BF)
    return pl.pallas_call(
        update_kernel,
        out_shape=[jax.ShapeDtypeStruct((height, width), BF)] + [jax.ShapeDtypeStruct((height // 4, width), BF)] * 3,
        in_specs=[smem, smem, smem, hbm, vmem, hbm, hbm],
        out_specs=[vmem] * 4,
        scratch_shapes=[held, held, pltpu.VMEM((NT * rank_pad, width), BF), pltpu.VMEM(q_rows.shape, BF), pltpu.VMEM(trailing.shape, BF), pltpu.SemaphoreType.DMA((41,))],
        compiler_params=pltpu.CompilerParams(vmem_limit_bytes=LIMIT << 20),
    )(
        x_at,
        left,
        upper,
        pltpu.with_memory_space_constraint(cols, pltpu.HBM),
        p_rows,
        pltpu.with_memory_space_constraint(q_rows, pltpu.HBM),
        pltpu.with_memory_space_constraint(trailing, pltpu.HBM),
    )


def body(trailing, left_outer, left_inner, upper_outer, upper_inner, left_ranks, upper_ranks):
    core_at = lax.axis_index("core")
    row_at = lax.axis_index("chip") * 2 + core_at
    x_at, z_at = lax.axis_index("xhi"), lax.axis_index("z")
    col_at = x_at * 16 + z_at
    half, depth = left_outer.shape

    mine = jnp.concatenate([left_outer, left_inner], axis=0)
    other = lax.ppermute(mine, "xhi", [(0, 1), (1, 0)])
    partner = lax.ppermute(upper_outer, "z", SWAP_Z)
    cols = lax.all_gather(jnp.concatenate([mine, other], axis=0), "z", axis=0, tiled=True)
    cols = cols.reshape(NT, 2, 2, half, -1)

    even = z_at % 2 == 0
    rows = jnp.concatenate(
        [jnp.where(even, upper_outer, partner), jnp.where(even, partner, upper_outer), upper_inner], axis=1
    )
    rows = lax.all_to_all(jnp.broadcast_to(rows[None], (NT // 2,) + rows.shape), "chip", 0, 0)
    across = lax.ppermute(rows, "core", [(0, 1), (1, 0)])
    lower = core_at == 0

    def whole(own, far):
        both = jnp.stack([jnp.where(lower, own, far), jnp.where(lower, far, own)], axis=1)
        return both.reshape((2, 8) + own.shape[1:])

    p_rows = whole(rows[..., :depth], across[..., :depth])
    q_rows = whole(rows[..., depth:], across[..., depth:])

    left = lax.dynamic_index_in_dim(left_ranks, row_at, 0, keepdims=False)
    upper = lax.dynamic_index_in_dim(upper_ranks, col_at // 2, 1, keepdims=False)
    updated, *parts = update(x_at.reshape(1).astype(jnp.int32), left, upper, cols, p_rows, q_rows, trailing)
    return updated, spread(updated, parts, col_at)


def solution(mesh):
    fine = Mesh(mesh.devices.reshape(8, 2, 2, 16), ("chip", "core", "xhi", "z"))
    grid = P(ROW, COL)
    turned = P(COL, ROW)
    return jax.shard_map(
        body,
        mesh=fine,
        in_specs=(grid, turned, turned, grid, grid, P(), P()),
        out_specs=(grid, P(ROW + COL, None)),
        check_vma=False,
    )
```

```python
import jax
import jax.numpy as jnp
from jax import lax
from jax.experimental import pallas as pl
from jax.experimental.pallas import tpu as pltpu
from jax.sharding import Mesh, PartitionSpec as P

NT = 16
ROW = ("chip", "core")
COL = ("xhi", "z")
BF = jnp.bfloat16
SWAP_Z = [(i, i ^ 1) for i in range(16)]
LIMIT = 20


def place(branches, default):
    for hit, value in branches:
        default = jnp.where(hit, value, default)
    return default


def spread(updated, parts, col_at):
    share = updated.shape[0] // 32
    sent = []
    for m in (3, 2, 1):
        block = lax.ppermute(parts[m - 1], COL, [(0, 8 * m), (1, 8 * m + 1)])
        sent.append((col_at // 8 == m, block))
    held = place(sent, updated[: 8 * share])
    spot = col_at % 8
    got = []
    for d in range(1, 8):
        piece = lax.dynamic_slice_in_dim(held, (spot + d) % 8 * share, share, 0)
        pairs = [(b + h, b + (h + d) % 8) for b in range(0, 32, 8) for h in (0, 1)]
        got.append(lax.ppermute(piece, COL, pairs))
    own = lax.dynamic_slice_in_dim(held, spot * share, share, 0)
    left = place([(spot == d, got[d - 1]) for d in range(1, 8)], own)
    right = place([((spot - 1) % 8 == d, got[d - 1]) for d in range(1, 8)], own)
    return jnp.concatenate([left, right], axis=1)


def update_kernel(
    left_ref, upper_ref, cols_ref, p_ref, q_ref, trailing_ref, out_ref, *rest
):
    parts, (outer_ref, inner_ref, weights_ref, q_held, dense_ref, sems) = rest[:3], rest[3:]
    rank_pad = p_ref.shape[2]
    depth = cols_ref.shape[4]
    copies = []

    def fetch(source, target):
        copies.append(pltpu.make_async_copy(source, target, sems.at[len(copies)]))

    for zz in range(8):
        for h in range(2):
            fetch(cols_ref.at[2 * zz + h, :, 1], inner_ref.at[zz, :, h])
        fetch(q_ref.at[:, zz], q_held.at[:, zz])
    for zz in range(8):
        for h in range(2):
            fetch(cols_ref.at[2 * zz + h, :, 0], outer_ref.at[zz, :, h])
    fetch(trailing_ref, dense_ref)
    for copy in copies:
        copy.start()
    t = lax.broadcasted_iota(jnp.int32, (rank_pad, rank_pad), 0)
    u = lax.broadcasted_iota(jnp.int32, (rank_pad, rank_pad), 1)
    for zz in range(8):
        for copy in copies[3 * zz : 3 * zz + 3]:
            copy.wait()
        for xhi in range(2):
            k = xhi * 8 + zz
            core = lax.dot_general(
                inner_ref[zz, xhi].reshape(rank_pad, depth),
                p_ref[xhi, zz],
                (((1,), (1,)), ((), ())),
                preferred_element_type=jnp.float32,
            )
            core = jnp.where((t < left_ref[k]) & (u < upper_ref[k]), core, 0.0).astype(BF)
            at = (2 * zz + xhi) * rank_pad
            weights_ref[at : at + rank_pad, :] = jnp.dot(
                core, q_held[xhi, zz], preferred_element_type=jnp.float32
            ).astype(BF)
    for copy in copies[24:]:
        copy.wait()
    outer = outer_ref[...].reshape(NT * rank_pad, depth)
    product = lax.dot_general(outer, weights_ref[...], (((0,), (0,)), ((), ())), preferred_element_type=jnp.float32)
    done = (dense_ref[...].astype(jnp.float32) - product).astype(BF)
    out_ref[...] = done
    part = done.shape[0] // 4
    for m in range(1, 4):
        parts[m - 1][...] = done[m * part : (m + 1) * part]


def update(left, upper, cols, p_rows, q_rows, trailing):
    height, width = trailing.shape
    rank_pad, depth, half = p_rows.shape[2], cols.shape[4], cols.shape[3]
    vmem, smem = pl.BlockSpec(memory_space=pltpu.VMEM), pl.BlockSpec(memory_space=pltpu.SMEM)
    hbm = pl.BlockSpec(memory_space=pltpu.HBM)
    held = pltpu.VMEM((8, 2, 2, half, depth), BF)
    return pl.pallas_call(
        update_kernel,
        out_shape=[jax.ShapeDtypeStruct((height, width), BF)] + [jax.ShapeDtypeStruct((height // 4, width), BF)] * 3,
        in_specs=[smem, smem, hbm, vmem, hbm, hbm],
        out_specs=[vmem] * 4,
        scratch_shapes=[held, held, pltpu.VMEM((NT * rank_pad, width), BF), pltpu.VMEM(q_rows.shape, BF), pltpu.VMEM(trailing.shape, BF), pltpu.SemaphoreType.DMA((41,))],
        compiler_params=pltpu.CompilerParams(vmem_limit_bytes=LIMIT << 20),
    )(
        left,
        upper,
        pltpu.with_memory_space_constraint(cols, pltpu.HBM),
        p_rows,
        pltpu.with_memory_space_constraint(q_rows, pltpu.HBM),
        pltpu.with_memory_space_constraint(trailing, pltpu.HBM),
    )


def body(trailing, left_outer, left_inner, upper_outer, upper_inner, left_ranks, upper_ranks):
    core_at = lax.axis_index("core")
    row_at = lax.axis_index("chip") * 2 + core_at
    x_at, z_at = lax.axis_index("xhi"), lax.axis_index("z")
    col_at = x_at * 16 + z_at
    half, depth = left_outer.shape

    both = jnp.concatenate([left_outer, left_inner], axis=0)
    both = lax.all_gather(both, "xhi", axis=0, tiled=True)
    partner = lax.ppermute(upper_outer, "z", SWAP_Z)
    cols = lax.all_gather(both, "z", axis=0, tiled=True)
    cols = cols.reshape(NT, 2, 2, half, -1)

    even = z_at % 2 == 0
    rows = jnp.concatenate(
        [jnp.where(even, upper_outer, partner), jnp.where(even, partner, upper_outer), upper_inner], axis=1
    )
    rows = lax.all_to_all(jnp.broadcast_to(rows[None], (NT // 2,) + rows.shape), "chip", 0, 0)
    across = lax.ppermute(rows, "core", [(0, 1), (1, 0)])
    lower = core_at == 0

    def whole(own, far):
        both = jnp.stack([jnp.where(lower, own, far), jnp.where(lower, far, own)], axis=1)
        return both.reshape((2, 8) + own.shape[1:])

    p_rows = whole(rows[..., :depth], across[..., :depth])
    q_rows = whole(rows[..., depth:], across[..., depth:])

    left = lax.dynamic_index_in_dim(left_ranks, row_at, 0, keepdims=False)
    upper = lax.dynamic_index_in_dim(upper_ranks, col_at // 2, 1, keepdims=False)
    updated, *parts = update(left, upper, cols, p_rows, q_rows, trailing)
    return updated, spread(updated, parts, col_at)


def solution(mesh):
    fine = Mesh(mesh.devices.reshape(8, 2, 2, 16), ("chip", "core", "xhi", "z"))
    grid = P(ROW, COL)
    turned = P(COL, ROW)
    return jax.shard_map(
        body,
        mesh=fine,
        in_specs=(grid, turned, turned, grid, grid, P(), P()),
        out_specs=(grid, P(ROW + COL, None)),
        check_vma=False,
    )
```

```python
import jax
import jax.numpy as jnp
from jax import lax
from jax.experimental import pallas as pl
from jax.experimental.pallas import tpu as pltpu
from jax.sharding import Mesh, PartitionSpec as P

NT = 16
ROW = ("chip", "core")
COL = ("xhi", "z")
BF = jnp.bfloat16
SWAP_Z = [(i, i ^ 1) for i in range(16)]
LIMIT = 20
SENT = (1, 3, 2)


def place(branches, default):
    for hit, value in branches:
        default = jnp.where(hit, value, default)
    return default


def spread(updated, parts, col_at):
    share = updated.shape[0] // 32
    sent = []
    for block, m in zip(parts, SENT):
        block = lax.ppermute(block, COL, [(0, 8 * m), (1, 8 * m + 1)])
        sent.append((col_at // 8 == m, block))
    held = place(sent, updated[: 8 * share])
    spot = col_at % 8
    got = []
    for d in range(1, 8):
        piece = lax.dynamic_slice_in_dim(held, (spot + d) % 8 * share, share, 0)
        pairs = [(b + h, b + (h + d) % 8) for b in range(0, 32, 8) for h in (0, 1)]
        got.append(lax.ppermute(piece, COL, pairs))
    own = lax.dynamic_slice_in_dim(held, spot * share, share, 0)
    left = place([(spot == d, got[d - 1]) for d in range(1, 8)], own)
    right = place([((spot - 1) % 8 == d, got[d - 1]) for d in range(1, 8)], own)
    return jnp.concatenate([left, right], axis=1)


def update_kernel(
    left_ref, upper_ref, cols_ref, p_ref, q_ref, trailing_ref, out_ref, *rest
):
    parts, (outer_ref, inner_ref, weights_ref, q_held, dense_ref, sems) = rest[:3], rest[3:]
    rank_pad = p_ref.shape[2]
    depth = cols_ref.shape[4]
    copies = []

    def fetch(source, target):
        copies.append(pltpu.make_async_copy(source, target, sems.at[len(copies)]))

    for zz in range(8):
        for h in range(2):
            fetch(cols_ref.at[2 * zz + h, :, 1], inner_ref.at[zz, :, h])
        fetch(q_ref.at[:, zz], q_held.at[:, zz])
    for zz in range(8):
        for h in range(2):
            fetch(cols_ref.at[2 * zz + h, :, 0], outer_ref.at[zz, :, h])
    fetch(trailing_ref, dense_ref)
    for copy in copies:
        copy.start()
    t = lax.broadcasted_iota(jnp.int32, (rank_pad, rank_pad), 0)
    u = lax.broadcasted_iota(jnp.int32, (rank_pad, rank_pad), 1)
    for zz in range(8):
        for copy in copies[3 * zz : 3 * zz + 3]:
            copy.wait()
        for xhi in range(2):
            k = xhi * 8 + zz
            core = lax.dot_general(
                inner_ref[zz, xhi].reshape(rank_pad, depth),
                p_ref[xhi, zz],
                (((1,), (1,)), ((), ())),
                preferred_element_type=jnp.float32,
            )
            core = jnp.where((t < left_ref[k]) & (u < upper_ref[k]), core, 0.0).astype(BF)
            at = (2 * zz + xhi) * rank_pad
            weights_ref[at : at + rank_pad, :] = jnp.dot(
                core, q_held[xhi, zz], preferred_element_type=jnp.float32
            ).astype(BF)
    for copy in copies[24:]:
        copy.wait()
    outer = outer_ref[...].reshape(NT * rank_pad, depth)
    product = lax.dot_general(outer, weights_ref[...], (((0,), (0,)), ((), ())), preferred_element_type=jnp.float32)
    done = (dense_ref[...].astype(jnp.float32) - product).astype(BF)
    out_ref[...] = done
    part = done.shape[0] // 4
    for part_ref, m in zip(parts, SENT):
        part_ref[...] = done[m * part : (m + 1) * part]


def update(left, upper, cols, p_rows, q_rows, trailing):
    height, width = trailing.shape
    rank_pad, depth, half = p_rows.shape[2], cols.shape[4], cols.shape[3]
    vmem, smem = pl.BlockSpec(memory_space=pltpu.VMEM), pl.BlockSpec(memory_space=pltpu.SMEM)
    hbm = pl.BlockSpec(memory_space=pltpu.HBM)
    held = pltpu.VMEM((8, 2, 2, half, depth), BF)
    return pl.pallas_call(
        update_kernel,
        out_shape=[jax.ShapeDtypeStruct((height, width), BF)] + [jax.ShapeDtypeStruct((height // 4, width), BF)] * 3,
        in_specs=[smem, smem, hbm, vmem, hbm, hbm],
        out_specs=[vmem] * 4,
        scratch_shapes=[held, held, pltpu.VMEM((NT * rank_pad, width), BF), pltpu.VMEM(q_rows.shape, BF), pltpu.VMEM(trailing.shape, BF), pltpu.SemaphoreType.DMA((41,))],
        compiler_params=pltpu.CompilerParams(vmem_limit_bytes=LIMIT << 20),
    )(
        left,
        upper,
        pltpu.with_memory_space_constraint(cols, pltpu.HBM),
        p_rows,
        pltpu.with_memory_space_constraint(q_rows, pltpu.HBM),
        pltpu.with_memory_space_constraint(trailing, pltpu.HBM),
    )


def body(trailing, left_outer, left_inner, upper_outer, upper_inner, left_ranks, upper_ranks):
    core_at = lax.axis_index("core")
    row_at = lax.axis_index("chip") * 2 + core_at
    x_at, z_at = lax.axis_index("xhi"), lax.axis_index("z")
    col_at = x_at * 16 + z_at
    half, depth = left_outer.shape

    both = jnp.concatenate([left_outer, left_inner], axis=0)
    both = lax.all_gather(both, "xhi", axis=0, tiled=True)
    partner = lax.ppermute(upper_outer, "z", SWAP_Z)
    cols = lax.all_gather(both, "z", axis=0, tiled=True)
    cols = cols.reshape(NT, 2, 2, half, -1)

    even = z_at % 2 == 0
    rows = jnp.concatenate(
        [jnp.where(even, upper_outer, partner), jnp.where(even, partner, upper_outer), upper_inner], axis=1
    )
    rows = lax.all_to_all(jnp.broadcast_to(rows[None], (NT // 2,) + rows.shape), "chip", 0, 0)
    across = lax.ppermute(rows, "core", [(0, 1), (1, 0)])
    lower = core_at == 0

    def whole(own, far):
        both = jnp.stack([jnp.where(lower, own, far), jnp.where(lower, far, own)], axis=1)
        return both.reshape((2, 8) + own.shape[1:])

    p_rows = whole(rows[..., :depth], across[..., :depth])
    q_rows = whole(rows[..., depth:], across[..., depth:])

    left = lax.dynamic_index_in_dim(left_ranks, row_at, 0, keepdims=False)
    upper = lax.dynamic_index_in_dim(upper_ranks, col_at // 2, 1, keepdims=False)
    updated, *parts = update(left, upper, cols, p_rows, q_rows, trailing)
    return updated, spread(updated, parts, col_at)


def solution(mesh):
    fine = Mesh(mesh.devices.reshape(8, 2, 2, 16), ("chip", "core", "xhi", "z"))
    grid = P(ROW, COL)
    turned = P(COL, ROW)
    return jax.shard_map(
        body,
        mesh=fine,
        in_specs=(grid, turned, turned, grid, grid, P(), P()),
        out_specs=(grid, P(ROW + COL, None)),
        check_vma=False,
    )
```

```python
import jax
import jax.numpy as jnp
from jax import lax
from jax.experimental import pallas as pl
from jax.experimental.pallas import tpu as pltpu
from jax.sharding import Mesh, PartitionSpec as P

NT = 16
ROW = ("chip", "core")
COL = ("xhi", "z")
BF = jnp.bfloat16
SWAP_Z = [(i, i ^ 1) for i in range(16)]
LIMIT = 20


def place(branches, default):
    for hit, value in branches:
        default = jnp.where(hit, value, default)
    return default


def spread(updated, parts, col_at):
    share = updated.shape[0] // 32
    sent = []
    for m in (3, 2, 1):
        block = lax.ppermute(parts[m - 1], COL, [(0, 8 * m), (1, 8 * m + 1)])
        sent.append((col_at // 8 == m, block))
    held = place(sent, updated[: 8 * share])
    spot = col_at % 8
    got = []
    for d in range(1, 8):
        piece = lax.dynamic_slice_in_dim(held, (spot + d) % 8 * share, share, 0)
        pairs = [(b + h, b + (h + d) % 8) for b in range(0, 32, 8) for h in (0, 1)]
        got.append(lax.ppermute(piece, COL, pairs))
    own = lax.dynamic_slice_in_dim(held, spot * share, share, 0)
    left = place([(spot == d, got[d - 1]) for d in range(1, 8)], own)
    right = place([((spot - 1) % 8 == d, got[d - 1]) for d in range(1, 8)], own)
    return jnp.concatenate([left, right], axis=1)


def update_kernel(
    left_ref, upper_ref, cols_ref, p_ref, q_ref, trailing_ref, out_ref, *rest
):
    parts, (outer_ref, inner_ref, weights_ref, q_held, dense_ref, sems) = rest[:3], rest[3:]
    rank_pad = p_ref.shape[2]
    depth = cols_ref.shape[4]
    copies = []

    def fetch(source, target):
        copies.append(pltpu.make_async_copy(source, target, sems.at[len(copies)]))

    needs = []
    for c in range(4):
        if c % 2 == 0:
            at = slice(2 * c, 2 * c + 4)
            fetch(q_ref.at[:, at], q_held.at[:, at])
        at = slice(4 * c, 4 * c + 4)
        fetch(cols_ref.at[at, :, 1], inner_ref.at[at])
        needs.append(len(copies))
    for c in range(2):
        at = slice(8 * c, 8 * c + 8)
        fetch(cols_ref.at[at, :, 0], outer_ref.at[at])
    fetch(trailing_ref, dense_ref)
    for copy in copies:
        copy.start()
    half = rank_pad // 2
    pair = (2 * rank_pad, 2 * rank_pad)
    t, u = lax.broadcasted_iota(jnp.int32, pair, 0), lax.broadcasted_iota(jnp.int32, pair, 1)
    u_low = u < rank_pad
    u = jnp.where(u_low, u, u - rank_pad)
    late = t >= rank_pad
    t = jnp.where(late, t - rank_pad, t)
    t_low = t < half
    t = jnp.where(t_low, t, t - half) + jnp.where(late, half, 0)
    same = t_low == u_low
    waited = 0
    for zz in range(8):
        while waited < needs[zz // 2]:
            copies[waited].wait()
            waited += 1
        core = lax.dot_general(
            inner_ref[2 * zz : 2 * zz + 2].reshape(2 * rank_pad, depth),
            jnp.concatenate([p_ref[0, zz], p_ref[1, zz]], axis=0),
            (((1,), (1,)), ((), ())),
            preferred_element_type=jnp.float32,
        )
        left_live = t < jnp.where(t_low, left_ref[zz], left_ref[zz + 8])
        upper_live = u < jnp.where(u_low, upper_ref[zz], upper_ref[zz + 8])
        core = jnp.where(same & left_live & upper_live, core, 0.0).astype(BF)
        at = 2 * zz * rank_pad
        weights_ref[at : at + 2 * rank_pad, :] = jnp.dot(
            core, jnp.concatenate([q_held[0, zz], q_held[1, zz]], axis=0), preferred_element_type=jnp.float32
        ).astype(BF)
    for copy in copies[waited:]:
        copy.wait()
    outer = outer_ref[...].reshape(NT * rank_pad, depth)
    product = lax.dot_general(outer, weights_ref[...], (((0,), (0,)), ((), ())), preferred_element_type=jnp.float32)
    done = (dense_ref[...].astype(jnp.float32) - product).astype(BF)
    out_ref[...] = done
    part = done.shape[0] // 4
    for m in range(1, 4):
        parts[m - 1][...] = done[m * part : (m + 1) * part]


def update(left, upper, cols, p_rows, q_rows, trailing):
    height, width = trailing.shape
    rank_pad, depth, half = p_rows.shape[2], cols.shape[4], cols.shape[3]
    vmem, smem = pl.BlockSpec(memory_space=pltpu.VMEM), pl.BlockSpec(memory_space=pltpu.SMEM)
    hbm = pl.BlockSpec(memory_space=pltpu.HBM)
    held = pltpu.VMEM((NT, 2, half, depth), BF)
    return pl.pallas_call(
        update_kernel,
        out_shape=[jax.ShapeDtypeStruct((height, width), BF)] + [jax.ShapeDtypeStruct((height // 4, width), BF)] * 3,
        in_specs=[smem, smem, hbm, vmem, hbm, hbm],
        out_specs=[vmem] * 4,
        scratch_shapes=[held, held, pltpu.VMEM((NT * rank_pad, width), BF), pltpu.VMEM(q_rows.shape, BF), pltpu.VMEM(trailing.shape, BF), pltpu.SemaphoreType.DMA((9,))],
        compiler_params=pltpu.CompilerParams(vmem_limit_bytes=LIMIT << 20),
    )(
        left,
        upper,
        pltpu.with_memory_space_constraint(cols, pltpu.HBM),
        p_rows,
        pltpu.with_memory_space_constraint(q_rows, pltpu.HBM),
        pltpu.with_memory_space_constraint(trailing, pltpu.HBM),
    )


def body(trailing, left_outer, left_inner, upper_outer, upper_inner, left_ranks, upper_ranks):
    core_at = lax.axis_index("core")
    row_at = lax.axis_index("chip") * 2 + core_at
    x_at, z_at = lax.axis_index("xhi"), lax.axis_index("z")
    col_at = x_at * 16 + z_at
    half, depth = left_outer.shape

    both = jnp.concatenate([left_outer, left_inner], axis=0)
    both = lax.all_gather(both, "xhi", axis=0, tiled=True)
    partner = lax.ppermute(upper_outer, "z", SWAP_Z)
    cols = lax.all_gather(both, "z", axis=0, tiled=True)
    cols = cols.reshape(NT, 2, 2, half, -1)

    even = z_at % 2 == 0
    rows = jnp.concatenate(
        [jnp.where(even, upper_outer, partner), jnp.where(even, partner, upper_outer), upper_inner], axis=1
    )
    rows = lax.all_to_all(jnp.broadcast_to(rows[None], (NT // 2,) + rows.shape), "chip", 0, 0)
    across = lax.ppermute(rows, "core", [(0, 1), (1, 0)])
    lower = core_at == 0

    def whole(own, far):
        both = jnp.stack([jnp.where(lower, own, far), jnp.where(lower, far, own)], axis=1)
        return both.reshape((2, 8) + own.shape[1:])

    p_rows = whole(rows[..., :depth], across[..., :depth])
    q_rows = whole(rows[..., depth:], across[..., depth:])

    left = lax.dynamic_index_in_dim(left_ranks, row_at, 0, keepdims=False)
    upper = lax.dynamic_index_in_dim(upper_ranks, col_at // 2, 1, keepdims=False)
    updated, *parts = update(left, upper, cols, p_rows, q_rows, trailing)
    return updated, spread(updated, parts, col_at)


def solution(mesh):
    fine = Mesh(mesh.devices.reshape(8, 2, 2, 16), ("chip", "core", "xhi", "z"))
    grid = P(ROW, COL)
    turned = P(COL, ROW)
    return jax.shard_map(
        body,
        mesh=fine,
        in_specs=(grid, turned, turned, grid, grid, P(), P()),
        out_specs=(grid, P(ROW + COL, None)),
        check_vma=False,
    )
```

```python
import jax
import jax.numpy as jnp
from jax import lax
from jax.experimental import pallas as pl
from jax.experimental.pallas import tpu as pltpu
from jax.sharding import Mesh, PartitionSpec as P

NT = 16
ROW = ("chip", "core")
COL = ("xhi", "z")
BF = jnp.bfloat16
SWAP_Z = [(i, i ^ 1) for i in range(16)]
LIMIT = 20


def place(branches, default):
    for hit, value in branches:
        default = jnp.where(hit, value, default)
    return default


def spread(updated, parts, col_at):
    share = updated.shape[0] // 32
    lands = (0, 6, 0, 6)
    sent = []
    for m in (3, 2, 1):
        block = lax.ppermute(parts[m - 1], COL, [(h, 8 * m + lands[m] + h) for h in (0, 1)])
        sent.append((col_at // 8 == m, block))
    held = place(sent, updated[: 8 * share])
    spot = col_at % 8
    got = []
    for d in range(1, 8):
        piece = lax.dynamic_slice_in_dim(held, (spot + d) % 8 * share, share, 0)
        pairs = [(8 * m + lands[m] + h, 8 * m + (lands[m] + h + d) % 8) for m in range(4) for h in (0, 1)]
        got.append(lax.ppermute(piece, COL, pairs))
    own = lax.dynamic_slice_in_dim(held, spot * share, share, 0)
    apart = (spot - jnp.where(col_at // 8 % 2 == 0, lands[0], lands[1])) % 8
    left = place([(apart == d, got[d - 1]) for d in range(1, 8)], own)
    right = place([((apart - 1) % 8 == d, got[d - 1]) for d in range(1, 8)], own)
    return jnp.concatenate([left, right], axis=1)


def update_kernel(
    left_ref, upper_ref, cols_ref, p_ref, q_ref, trailing_ref, out_ref, *rest
):
    parts, (outer_ref, inner_ref, weights_ref, q_held, dense_ref, sems) = rest[:3], rest[3:]
    rank_pad = p_ref.shape[2]
    depth = cols_ref.shape[4]
    copies = []

    def fetch(source, target):
        copies.append(pltpu.make_async_copy(source, target, sems.at[len(copies)]))

    needs = []
    for c in range(4):
        if c % 2 == 0:
            at = slice(2 * c, 2 * c + 4)
            fetch(q_ref.at[:, at], q_held.at[:, at])
        at = slice(4 * c, 4 * c + 4)
        fetch(cols_ref.at[at, :, 1], inner_ref.at[at])
        needs.append(len(copies))
    for c in range(2):
        at = slice(8 * c, 8 * c + 8)
        fetch(cols_ref.at[at, :, 0], outer_ref.at[at])
    fetch(trailing_ref, dense_ref)
    for copy in copies:
        copy.start()
    half = rank_pad // 2
    pair = (2 * rank_pad, 2 * rank_pad)
    t, u = lax.broadcasted_iota(jnp.int32, pair, 0), lax.broadcasted_iota(jnp.int32, pair, 1)
    u_low = u < rank_pad
    u = jnp.where(u_low, u, u - rank_pad)
    late = t >= rank_pad
    t = jnp.where(late, t - rank_pad, t)
    t_low = t < half
    t = jnp.where(t_low, t, t - half) + jnp.where(late, half, 0)
    same = t_low == u_low
    waited = 0
    for zz in range(8):
        while waited < needs[zz // 2]:
            copies[waited].wait()
            waited += 1
        core = lax.dot_general(
            inner_ref[2 * zz : 2 * zz + 2].reshape(2 * rank_pad, depth),
            jnp.concatenate([p_ref[0, zz], p_ref[1, zz]], axis=0),
            (((1,), (1,)), ((), ())),
            preferred_element_type=jnp.float32,
        )
        left_live = t < jnp.where(t_low, left_ref[zz], left_ref[zz + 8])
        upper_live = u < jnp.where(u_low, upper_ref[zz], upper_ref[zz + 8])
        core = jnp.where(same & left_live & upper_live, core, 0.0).astype(BF)
        at = 2 * zz * rank_pad
        weights_ref[at : at + 2 * rank_pad, :] = jnp.dot(
            core, jnp.concatenate([q_held[0, zz], q_held[1, zz]], axis=0), preferred_element_type=jnp.float32
        ).astype(BF)
    for copy in copies[waited:]:
        copy.wait()
    outer = outer_ref[...].reshape(NT * rank_pad, depth)
    product = lax.dot_general(outer, weights_ref[...], (((0,), (0,)), ((), ())), preferred_element_type=jnp.float32)
    done = (dense_ref[...].astype(jnp.float32) - product).astype(BF)
    out_ref[...] = done
    part = done.shape[0] // 4
    for m in range(1, 4):
        parts[m - 1][...] = done[m * part : (m + 1) * part]


def update(left, upper, cols, p_rows, q_rows, trailing):
    height, width = trailing.shape
    rank_pad, depth, half = p_rows.shape[2], cols.shape[4], cols.shape[3]
    vmem, smem = pl.BlockSpec(memory_space=pltpu.VMEM), pl.BlockSpec(memory_space=pltpu.SMEM)
    hbm = pl.BlockSpec(memory_space=pltpu.HBM)
    held = pltpu.VMEM((NT, 2, half, depth), BF)
    return pl.pallas_call(
        update_kernel,
        out_shape=[jax.ShapeDtypeStruct((height, width), BF)] + [jax.ShapeDtypeStruct((height // 4, width), BF)] * 3,
        in_specs=[smem, smem, hbm, vmem, hbm, hbm],
        out_specs=[vmem] * 4,
        scratch_shapes=[held, held, pltpu.VMEM((NT * rank_pad, width), BF), pltpu.VMEM(q_rows.shape, BF), pltpu.VMEM(trailing.shape, BF), pltpu.SemaphoreType.DMA((9,))],
        compiler_params=pltpu.CompilerParams(vmem_limit_bytes=LIMIT << 20),
    )(
        left,
        upper,
        pltpu.with_memory_space_constraint(cols, pltpu.HBM),
        p_rows,
        pltpu.with_memory_space_constraint(q_rows, pltpu.HBM),
        pltpu.with_memory_space_constraint(trailing, pltpu.HBM),
    )


def body(trailing, left_outer, left_inner, upper_outer, upper_inner, left_ranks, upper_ranks):
    core_at = lax.axis_index("core")
    row_at = lax.axis_index("chip") * 2 + core_at
    x_at, z_at = lax.axis_index("xhi"), lax.axis_index("z")
    col_at = x_at * 16 + z_at
    half, depth = left_outer.shape

    both = jnp.concatenate([left_outer, left_inner], axis=0)
    both = lax.all_gather(both, "xhi", axis=0, tiled=True)
    partner = lax.ppermute(upper_outer, "z", SWAP_Z)
    cols = lax.all_gather(both, "z", axis=0, tiled=True)
    cols = cols.reshape(NT, 2, 2, half, -1)

    even = z_at % 2 == 0
    rows = jnp.concatenate(
        [jnp.where(even, upper_outer, partner), jnp.where(even, partner, upper_outer), upper_inner], axis=1
    )
    rows = lax.all_to_all(jnp.broadcast_to(rows[None], (NT // 2,) + rows.shape), "chip", 0, 0)
    across = lax.ppermute(rows, "core", [(0, 1), (1, 0)])
    lower = core_at == 0

    def whole(own, far):
        both = jnp.stack([jnp.where(lower, own, far), jnp.where(lower, far, own)], axis=1)
        return both.reshape((2, 8) + own.shape[1:])

    p_rows = whole(rows[..., :depth], across[..., :depth])
    q_rows = whole(rows[..., depth:], across[..., depth:])

    left = lax.dynamic_index_in_dim(left_ranks, row_at, 0, keepdims=False)
    upper = lax.dynamic_index_in_dim(upper_ranks, col_at // 2, 1, keepdims=False)
    updated, *parts = update(left, upper, cols, p_rows, q_rows, trailing)
    return updated, spread(updated, parts, col_at)


def solution(mesh):
    fine = Mesh(mesh.devices.reshape(8, 2, 2, 16), ("chip", "core", "xhi", "z"))
    grid = P(ROW, COL)
    turned = P(COL, ROW)
    return jax.shard_map(
        body,
        mesh=fine,
        in_specs=(grid, turned, turned, grid, grid, P(), P()),
        out_specs=(grid, P(ROW + COL, None)),
        check_vma=False,
    )
```

```python
import jax
import jax.numpy as jnp
from jax import lax
from jax.experimental import pallas as pl
from jax.experimental.pallas import tpu as pltpu
from jax.sharding import Mesh, PartitionSpec as P

NT = 16
ROW = ("chip", "core")
COL = ("xhi", "z")
BF = jnp.bfloat16
SWAP_Z = [(i, i ^ 1) for i in range(16)]
LIMIT = 20


def place(branches, default):
    for hit, value in branches:
        default = jnp.where(hit, value, default)
    return default


LANDS = (4, 7, 4, 7)


def column_of(group, pos):
    return group // 2 * 16 + (group % 2 * 8 + pos - 4) % 16


def spread(parts, x_at, z_at):
    share = parts[0].shape[0] // 8
    turned = (z_at + 4) % 16
    group, pos = x_at * 2 + turned // 8, turned % 8
    landing = [[(LANDS[m] + h) % 8 for h in (0, 1)] for m in range(4)]
    sent = []
    for m in (3, 2, 1):
        block = lax.ppermute(parts[m], COL, [(h, column_of(m, landing[m][h])) for h in (0, 1)])
        sent.append((group == m, block))
    held = place(sent, parts[0])
    got = []
    for d in range(1, 8):
        piece = lax.dynamic_slice_in_dim(held, (pos + d) % 8 * share, share, 0)
        pairs = [(column_of(m, at), column_of(m, (at + d) % 8)) for m in range(4) for at in landing[m]]
        got.append(lax.ppermute(piece, COL, pairs))
    own = lax.dynamic_slice_in_dim(held, pos * share, share, 0)
    apart = (pos - jnp.where(group % 2 == 0, LANDS[0], LANDS[1])) % 8
    left = place([(apart == d, got[d - 1]) for d in range(1, 8)], own)
    right = place([((apart - 1) % 8 == d, got[d - 1]) for d in range(1, 8)], own)
    return jnp.concatenate([left, right], axis=1)


def update_kernel(
    left_ref, upper_ref, cols_ref, p_ref, q_ref, trailing_ref, out_ref, *rest
):
    parts, (outer_ref, inner_ref, weights_ref, q_held, dense_ref, sems) = rest[:4], rest[4:]
    rank_pad = p_ref.shape[2]
    depth = cols_ref.shape[4]
    copies = []

    def fetch(source, target):
        copies.append(pltpu.make_async_copy(source, target, sems.at[len(copies)]))

    needs = []
    for c in range(4):
        if c % 2 == 0:
            at = slice(2 * c, 2 * c + 4)
            fetch(q_ref.at[:, at], q_held.at[:, at])
        at = slice(4 * c, 4 * c + 4)
        fetch(cols_ref.at[at, :, 1], inner_ref.at[at])
        needs.append(len(copies))
    for c in range(2):
        at = slice(8 * c, 8 * c + 8)
        fetch(cols_ref.at[at, :, 0], outer_ref.at[at])
    fetch(trailing_ref, dense_ref)
    for copy in copies:
        copy.start()
    half = rank_pad // 2
    pair = (2 * rank_pad, 2 * rank_pad)
    t, u = lax.broadcasted_iota(jnp.int32, pair, 0), lax.broadcasted_iota(jnp.int32, pair, 1)
    u_low = u < rank_pad
    u = jnp.where(u_low, u, u - rank_pad)
    late = t >= rank_pad
    t = jnp.where(late, t - rank_pad, t)
    t_low = t < half
    t = jnp.where(t_low, t, t - half) + jnp.where(late, half, 0)
    same = t_low == u_low
    waited = 0
    for zz in range(8):
        while waited < needs[zz // 2]:
            copies[waited].wait()
            waited += 1
        core = lax.dot_general(
            inner_ref[2 * zz : 2 * zz + 2].reshape(2 * rank_pad, depth),
            jnp.concatenate([p_ref[0, zz], p_ref[1, zz]], axis=0),
            (((1,), (1,)), ((), ())),
            preferred_element_type=jnp.float32,
        )
        left_live = t < jnp.where(t_low, left_ref[zz], left_ref[zz + 8])
        upper_live = u < jnp.where(u_low, upper_ref[zz], upper_ref[zz + 8])
        core = jnp.where(same & left_live & upper_live, core, 0.0).astype(BF)
        at = 2 * zz * rank_pad
        weights_ref[at : at + 2 * rank_pad, :] = jnp.dot(
            core, jnp.concatenate([q_held[0, zz], q_held[1, zz]], axis=0), preferred_element_type=jnp.float32
        ).astype(BF)
    for copy in copies[waited:]:
        copy.wait()
    outer = outer_ref[...].reshape(NT * rank_pad, depth)
    product = lax.dot_general(outer, weights_ref[...], (((0,), (0,)), ((), ())), preferred_element_type=jnp.float32)
    done = (dense_ref[...].astype(jnp.float32) - product).astype(BF)
    out_ref[...] = done
    share = done.shape[0] // 32
    for m, part_ref in enumerate(parts):
        for pos in range(8):
            at = column_of(m, pos) * share
            part_ref[pos * share : (pos + 1) * share, :] = done[at : at + share]


def update(left, upper, cols, p_rows, q_rows, trailing):
    height, width = trailing.shape
    rank_pad, depth, half = p_rows.shape[2], cols.shape[4], cols.shape[3]
    vmem, smem = pl.BlockSpec(memory_space=pltpu.VMEM), pl.BlockSpec(memory_space=pltpu.SMEM)
    hbm = pl.BlockSpec(memory_space=pltpu.HBM)
    held = pltpu.VMEM((NT, 2, half, depth), BF)
    return pl.pallas_call(
        update_kernel,
        out_shape=[jax.ShapeDtypeStruct((height, width), BF)] + [jax.ShapeDtypeStruct((height // 4, width), BF)] * 4,
        in_specs=[smem, smem, hbm, vmem, hbm, hbm],
        out_specs=[vmem] * 5,
        scratch_shapes=[held, held, pltpu.VMEM((NT * rank_pad, width), BF), pltpu.VMEM(q_rows.shape, BF), pltpu.VMEM(trailing.shape, BF), pltpu.SemaphoreType.DMA((9,))],
        compiler_params=pltpu.CompilerParams(vmem_limit_bytes=LIMIT << 20),
    )(
        left,
        upper,
        pltpu.with_memory_space_constraint(cols, pltpu.HBM),
        p_rows,
        pltpu.with_memory_space_constraint(q_rows, pltpu.HBM),
        pltpu.with_memory_space_constraint(trailing, pltpu.HBM),
    )


def body(trailing, left_outer, left_inner, upper_outer, upper_inner, left_ranks, upper_ranks):
    core_at = lax.axis_index("core")
    row_at = lax.axis_index("chip") * 2 + core_at
    x_at, z_at = lax.axis_index("xhi"), lax.axis_index("z")
    col_at = x_at * 16 + z_at
    half, depth = left_outer.shape

    both = jnp.concatenate([left_outer, left_inner], axis=0)
    both = lax.all_gather(both, "xhi", axis=0, tiled=True)
    partner = lax.ppermute(upper_outer, "z", SWAP_Z)
    cols = lax.all_gather(both, "z", axis=0, tiled=True)
    cols = cols.reshape(NT, 2, 2, half, -1)

    even = z_at % 2 == 0
    rows = jnp.concatenate(
        [jnp.where(even, upper_outer, partner), jnp.where(even, partner, upper_outer), upper_inner], axis=1
    )
    rows = lax.all_to_all(jnp.broadcast_to(rows[None], (NT // 2,) + rows.shape), "chip", 0, 0)
    across = lax.ppermute(rows, "core", [(0, 1), (1, 0)])
    lower = core_at == 0

    def whole(own, far):
        both = jnp.stack([jnp.where(lower, own, far), jnp.where(lower, far, own)], axis=1)
        return both.reshape((2, 8) + own.shape[1:])

    p_rows = whole(rows[..., :depth], across[..., :depth])
    q_rows = whole(rows[..., depth:], across[..., depth:])

    left = lax.dynamic_index_in_dim(left_ranks, row_at, 0, keepdims=False)
    upper = lax.dynamic_index_in_dim(upper_ranks, col_at // 2, 1, keepdims=False)
    updated, *parts = update(left, upper, cols, p_rows, q_rows, trailing)
    return updated, spread(parts, x_at, z_at)


def solution(mesh):
    fine = Mesh(mesh.devices.reshape(8, 2, 2, 16), ("chip", "core", "xhi", "z"))
    grid = P(ROW, COL)
    turned = P(COL, ROW)
    return jax.shard_map(
        body,
        mesh=fine,
        in_specs=(grid, turned, turned, grid, grid, P(), P()),
        out_specs=(grid, P(ROW + COL, None)),
        check_vma=False,
    )
```

```python
import jax
import jax.numpy as jnp
from jax import lax
from jax.experimental import pallas as pl
from jax.experimental.pallas import tpu as pltpu
from jax.sharding import Mesh, PartitionSpec as P

NT = 16
ROW = ("chip", "core")
COL = ("xhi", "z")
BF = jnp.bfloat16
SWAP_Z = [(i, i ^ 1) for i in range(16)]
LIMIT = 20


def place(branches, default):
    for hit, value in branches:
        default = jnp.where(hit, value, default)
    return default


LANDS = (4, 7, 4, 7)
STEPS = (3, 2, 7, 1, 6, 5, 4)


def column_of(group, pos):
    return group // 2 * 16 + (group % 2 * 8 + pos - 4) % 16


def spread(parts, x_at, z_at):
    share = parts[0].shape[0] // 8
    turned = (z_at + 4) % 16
    group, pos = x_at * 2 + turned // 8, turned % 8
    landing = [[(LANDS[m] + h) % 8 for h in (0, 1)] for m in range(4)]
    sent = []
    for m in (2, 1, 3):
        block = lax.ppermute(parts[m], COL, [(h, column_of(m, landing[m][h])) for h in (0, 1)])
        sent.append((group == m, block))
    held = place(sent, parts[0])
    got = {}
    for d in STEPS:
        piece = lax.dynamic_slice_in_dim(held, (pos + d) % 8 * share, share, 0)
        pairs = [(column_of(m, at), column_of(m, (at + d) % 8)) for m in range(4) for at in landing[m]]
        got[d] = lax.ppermute(piece, COL, pairs)
    own = lax.dynamic_slice_in_dim(held, pos * share, share, 0)
    apart = (pos - jnp.where(group % 2 == 0, LANDS[0], LANDS[1])) % 8
    left = place([(apart == d, got[d]) for d in STEPS], own)
    right = place([((apart - 1) % 8 == d, got[d]) for d in STEPS], own)
    return jnp.concatenate([left, right], axis=1)


def update_kernel(
    left_ref, upper_ref, cols_ref, p_ref, q_ref, trailing_ref, out_ref, *rest
):
    parts, (outer_ref, inner_ref, weights_ref, q_held, dense_ref, sems) = rest[:4], rest[4:]
    rank_pad = p_ref.shape[2]
    depth = cols_ref.shape[4]
    copies = []

    def fetch(source, target):
        copies.append(pltpu.make_async_copy(source, target, sems.at[len(copies)]))

    needs = []
    for c in range(4):
        if c % 2 == 0:
            at = slice(2 * c, 2 * c + 4)
            fetch(q_ref.at[:, at], q_held.at[:, at])
        at = slice(4 * c, 4 * c + 4)
        fetch(cols_ref.at[at, :, 1], inner_ref.at[at])
        needs.append(len(copies))
    for c in range(2):
        at = slice(8 * c, 8 * c + 8)
        fetch(cols_ref.at[at, :, 0], outer_ref.at[at])
    fetch(trailing_ref, dense_ref)
    for copy in copies:
        copy.start()
    half = rank_pad // 2
    pair = (2 * rank_pad, 2 * rank_pad)
    t, u = lax.broadcasted_iota(jnp.int32, pair, 0), lax.broadcasted_iota(jnp.int32, pair, 1)
    u_low = u < rank_pad
    u = jnp.where(u_low, u, u - rank_pad)
    late = t >= rank_pad
    t = jnp.where(late, t - rank_pad, t)
    t_low = t < half
    t = jnp.where(t_low, t, t - half) + jnp.where(late, half, 0)
    same = t_low == u_low
    waited = 0
    for zz in range(8):
        while waited < needs[zz // 2]:
            copies[waited].wait()
            waited += 1
        core = lax.dot_general(
            inner_ref[2 * zz : 2 * zz + 2].reshape(2 * rank_pad, depth),
            jnp.concatenate([p_ref[0, zz], p_ref[1, zz]], axis=0),
            (((1,), (1,)), ((), ())),
            preferred_element_type=jnp.float32,
        )
        left_live = t < jnp.where(t_low, left_ref[zz], left_ref[zz + 8])
        upper_live = u < jnp.where(u_low, upper_ref[zz], upper_ref[zz + 8])
        core = jnp.where(same & left_live & upper_live, core, 0.0).astype(BF)
        at = 2 * zz * rank_pad
        weights_ref[at : at + 2 * rank_pad, :] = jnp.dot(
            core, jnp.concatenate([q_held[0, zz], q_held[1, zz]], axis=0), preferred_element_type=jnp.float32
        ).astype(BF)
    for copy in copies[waited:]:
        copy.wait()
    outer = outer_ref[...].reshape(NT * rank_pad, depth)
    product = lax.dot_general(outer, weights_ref[...], (((0,), (0,)), ((), ())), preferred_element_type=jnp.float32)
    done = (dense_ref[...].astype(jnp.float32) - product).astype(BF)
    out_ref[...] = done
    share = done.shape[0] // 32
    for m, part_ref in enumerate(parts):
        for pos in range(8):
            at = column_of(m, pos) * share
            part_ref[pos * share : (pos + 1) * share, :] = done[at : at + share]


def update(left, upper, cols, p_rows, q_rows, trailing):
    height, width = trailing.shape
    rank_pad, depth, half = p_rows.shape[2], cols.shape[4], cols.shape[3]
    vmem, smem = pl.BlockSpec(memory_space=pltpu.VMEM), pl.BlockSpec(memory_space=pltpu.SMEM)
    hbm = pl.BlockSpec(memory_space=pltpu.HBM)
    held = pltpu.VMEM((NT, 2, half, depth), BF)
    return pl.pallas_call(
        update_kernel,
        out_shape=[jax.ShapeDtypeStruct((height, width), BF)] + [jax.ShapeDtypeStruct((height // 4, width), BF)] * 4,
        in_specs=[smem, smem, hbm, vmem, hbm, hbm],
        out_specs=[vmem] * 5,
        scratch_shapes=[held, held, pltpu.VMEM((NT * rank_pad, width), BF), pltpu.VMEM(q_rows.shape, BF), pltpu.VMEM(trailing.shape, BF), pltpu.SemaphoreType.DMA((9,))],
        compiler_params=pltpu.CompilerParams(vmem_limit_bytes=LIMIT << 20),
    )(
        left,
        upper,
        pltpu.with_memory_space_constraint(cols, pltpu.HBM),
        p_rows,
        pltpu.with_memory_space_constraint(q_rows, pltpu.HBM),
        pltpu.with_memory_space_constraint(trailing, pltpu.HBM),
    )


def body(trailing, left_outer, left_inner, upper_outer, upper_inner, left_ranks, upper_ranks):
    core_at = lax.axis_index("core")
    row_at = lax.axis_index("chip") * 2 + core_at
    x_at, z_at = lax.axis_index("xhi"), lax.axis_index("z")
    col_at = x_at * 16 + z_at
    half, depth = left_outer.shape

    both = jnp.concatenate([left_outer, left_inner], axis=0)
    both = lax.all_gather(both, "xhi", axis=0, tiled=True)
    partner = lax.ppermute(upper_outer, "z", SWAP_Z)
    cols = lax.all_gather(both, "z", axis=0, tiled=True)
    cols = cols.reshape(NT, 2, 2, half, -1)

    even = z_at % 2 == 0
    rows = jnp.concatenate(
        [jnp.where(even, upper_outer, partner), jnp.where(even, partner, upper_outer), upper_inner], axis=1
    )
    rows = lax.all_to_all(jnp.broadcast_to(rows[None], (NT // 2,) + rows.shape), "chip", 0, 0)
    across = lax.ppermute(rows, "core", [(0, 1), (1, 0)])
    lower = core_at == 0

    def whole(own, far):
        both = jnp.stack([jnp.where(lower, own, far), jnp.where(lower, far, own)], axis=1)
        return both.reshape((2, 8) + own.shape[1:])

    p_rows = whole(rows[..., :depth], across[..., :depth])
    q_rows = whole(rows[..., depth:], across[..., depth:])

    left = lax.dynamic_index_in_dim(left_ranks, row_at, 0, keepdims=False)
    upper = lax.dynamic_index_in_dim(upper_ranks, col_at // 2, 1, keepdims=False)
    updated, *parts = update(left, upper, cols, p_rows, q_rows, trailing)
    return updated, spread(parts, x_at, z_at)


def solution(mesh):
    fine = Mesh(mesh.devices.reshape(8, 2, 2, 16), ("chip", "core", "xhi", "z"))
    grid = P(ROW, COL)
    turned = P(COL, ROW)
    return jax.shard_map(
        body,
        mesh=fine,
        in_specs=(grid, turned, turned, grid, grid, P(), P()),
        out_specs=(grid, P(ROW + COL, None)),
        check_vma=False,
    )
```

```python
import jax
import jax.numpy as jnp
from jax import lax
from jax.experimental import pallas as pl
from jax.experimental.pallas import tpu as pltpu
from jax.sharding import Mesh, PartitionSpec as P

NT = 16
ROW = ("chip", "core")
COL = ("xhi", "z")
BF = jnp.bfloat16
SWAP_Z = [(i, i ^ 1) for i in range(16)]
LIMIT = 20


def place(branches, default):
    for hit, value in branches:
        default = jnp.where(hit, value, default)
    return default


LANDS = (4, 7, 4, 7)
STEPS = (3, 2, 7, 1, 6, 5, 4)


def column_of(group, pos):
    return group // 2 * 16 + (group % 2 * 8 + pos - 4) % 16


def spread(parts, x_at, z_at):
    share = parts[0].shape[0] // 8
    turned = (z_at + 4) % 16
    group, pos = x_at * 2 + turned // 8, turned % 8
    landing = [[(LANDS[m] + h) % 8 for h in (0, 1)] for m in range(4)]
    sent = []
    for m in (3, 2, 1):
        block = lax.ppermute(parts[m], COL, [(h, column_of(m, landing[m][h])) for h in (0, 1)])
        sent.append((group == m, block))
    held = place(sent, parts[0])
    got = {}
    for d in STEPS:
        piece = lax.dynamic_slice_in_dim(held, (pos + d) % 8 * share, share, 0)
        pairs = [(column_of(m, at), column_of(m, (at + d) % 8)) for m in range(4) for at in landing[m]]
        got[d] = lax.ppermute(piece, COL, pairs)
    own = lax.dynamic_slice_in_dim(held, pos * share, share, 0)
    apart = (pos - jnp.where(group % 2 == 0, LANDS[0], LANDS[1])) % 8
    left = place([(apart == d, got[d]) for d in STEPS], own)
    right = place([((apart - 1) % 8 == d, got[d]) for d in STEPS], own)
    return jnp.concatenate([left, right], axis=1)


def update_kernel(
    left_ref, upper_ref, cols_ref, p_ref, q_ref, trailing_ref, out_ref, *rest
):
    parts, (outer_ref, inner_ref, weights_ref, q_held, dense_ref, sems) = rest[:4], rest[4:]
    rank_pad = p_ref.shape[2]
    depth = cols_ref.shape[4]
    copies = []

    def fetch(source, target):
        copies.append(pltpu.make_async_copy(source, target, sems.at[len(copies)]))

    needs = []
    for c in range(4):
        if c % 2 == 0:
            at = slice(2 * c, 2 * c + 4)
            fetch(q_ref.at[:, at], q_held.at[:, at])
        at = slice(4 * c, 4 * c + 4)
        fetch(cols_ref.at[at, :, 1], inner_ref.at[at])
        needs.append(len(copies))
    for c in range(2):
        at = slice(8 * c, 8 * c + 8)
        fetch(cols_ref.at[at, :, 0], outer_ref.at[at])
    fetch(trailing_ref, dense_ref)
    for copy in copies:
        copy.start()
    half = rank_pad // 2
    pair = (2 * rank_pad, 2 * rank_pad)
    t, u = lax.broadcasted_iota(jnp.int32, pair, 0), lax.broadcasted_iota(jnp.int32, pair, 1)
    u_low = u < rank_pad
    u = jnp.where(u_low, u, u - rank_pad)
    late = t >= rank_pad
    t = jnp.where(late, t - rank_pad, t)
    t_low = t < half
    t = jnp.where(t_low, t, t - half) + jnp.where(late, half, 0)
    same = t_low == u_low
    waited = 0
    for zz in range(8):
        while waited < needs[zz // 2]:
            copies[waited].wait()
            waited += 1
        core = lax.dot_general(
            inner_ref[2 * zz : 2 * zz + 2].reshape(2 * rank_pad, depth),
            jnp.concatenate([p_ref[0, zz], p_ref[1, zz]], axis=0),
            (((1,), (1,)), ((), ())),
            preferred_element_type=jnp.float32,
        )
        left_live = t < jnp.where(t_low, left_ref[zz], left_ref[zz + 8])
        upper_live = u < jnp.where(u_low, upper_ref[zz], upper_ref[zz + 8])
        core = jnp.where(same & left_live & upper_live, core, 0.0).astype(BF)
        at = 2 * zz * rank_pad
        weights_ref[at : at + 2 * rank_pad, :] = jnp.dot(
            core, jnp.concatenate([q_held[0, zz], q_held[1, zz]], axis=0), preferred_element_type=jnp.float32
        ).astype(BF)
    for copy in copies[waited:]:
        copy.wait()
    outer = outer_ref[...].reshape(NT * rank_pad, depth)
    product = lax.dot_general(outer, weights_ref[...], (((0,), (0,)), ((), ())), preferred_element_type=jnp.float32)
    done = (dense_ref[...].astype(jnp.float32) - product).astype(BF)
    out_ref[...] = done
    share = done.shape[0] // 32
    for m, part_ref in enumerate(parts):
        for pos in range(8):
            at = column_of(m, pos) * share
            part_ref[pos * share : (pos + 1) * share, :] = done[at : at + share]


def update(left, upper, cols, p_rows, q_rows, trailing):
    height, width = trailing.shape
    rank_pad, depth, half = p_rows.shape[2], cols.shape[4], cols.shape[3]
    vmem, smem = pl.BlockSpec(memory_space=pltpu.VMEM), pl.BlockSpec(memory_space=pltpu.SMEM)
    hbm = pl.BlockSpec(memory_space=pltpu.HBM)
    held = pltpu.VMEM((NT, 2, half, depth), BF)
    return pl.pallas_call(
        update_kernel,
        out_shape=[jax.ShapeDtypeStruct((height, width), BF)] + [jax.ShapeDtypeStruct((height // 4, width), BF)] * 4,
        in_specs=[smem, smem, hbm, vmem, hbm, hbm],
        out_specs=[vmem] * 5,
        scratch_shapes=[held, held, pltpu.VMEM((NT * rank_pad, width), BF), pltpu.VMEM(q_rows.shape, BF), pltpu.VMEM(trailing.shape, BF), pltpu.SemaphoreType.DMA((9,))],
        compiler_params=pltpu.CompilerParams(vmem_limit_bytes=LIMIT << 20),
    )(
        left,
        upper,
        pltpu.with_memory_space_constraint(cols, pltpu.HBM),
        p_rows,
        pltpu.with_memory_space_constraint(q_rows, pltpu.HBM),
        pltpu.with_memory_space_constraint(trailing, pltpu.HBM),
    )


def body(trailing, left_outer, left_inner, upper_outer, upper_inner, left_ranks, upper_ranks):
    core_at = lax.axis_index("core")
    row_at = lax.axis_index("chip") * 2 + core_at
    x_at, z_at = lax.axis_index("xhi"), lax.axis_index("z")
    col_at = x_at * 16 + z_at
    half, depth = left_outer.shape

    both = jnp.concatenate([left_outer, left_inner], axis=0)
    both = lax.all_gather(both, "xhi", axis=0, tiled=True)
    partner = lax.ppermute(upper_outer, "z", SWAP_Z)
    cols = lax.all_gather(both, "z", axis=0, tiled=True)
    cols = cols.reshape(NT, 2, 2, half, -1)

    even = z_at % 2 == 0
    rows = jnp.concatenate(
        [jnp.where(even, upper_outer, partner), jnp.where(even, partner, upper_outer), upper_inner], axis=1
    )
    rows = lax.all_to_all(jnp.broadcast_to(rows[None], (NT // 2,) + rows.shape), "chip", 0, 0)
    across = lax.ppermute(rows, "core", [(0, 1), (1, 0)])
    lower = core_at == 0

    def whole(own, far):
        both = jnp.stack([jnp.where(lower, own, far), jnp.where(lower, far, own)], axis=1)
        return both.reshape((2, 8) + own.shape[1:])

    p_rows = whole(rows[..., :depth], across[..., :depth])
    q_rows = whole(rows[..., depth:], across[..., depth:])

    left = lax.dynamic_index_in_dim(left_ranks, row_at, 0, keepdims=False)
    upper = lax.dynamic_index_in_dim(upper_ranks, col_at // 2, 1, keepdims=False)
    updated, *parts = update(left, upper, cols, p_rows, q_rows, trailing)
    return updated, spread(parts, x_at, z_at)


def solution(mesh):
    fine = Mesh(mesh.devices.reshape(8, 2, 2, 16), ("chip", "core", "xhi", "z"))
    grid = P(ROW, COL)
    turned = P(COL, ROW)
    return jax.shard_map(
        body,
        mesh=fine,
        in_specs=(grid, turned, turned, grid, grid, P(), P()),
        out_specs=(grid, P(ROW + COL, None)),
        check_vma=False,
    )
```

```python
import jax
import jax.numpy as jnp
from jax import lax
from jax.experimental import pallas as pl
from jax.experimental.pallas import tpu as pltpu
from jax.sharding import Mesh, PartitionSpec as P

NT = 16
ROW = ("chip", "core")
COL = ("xhi", "z")
BF = jnp.bfloat16
SWAP_Z = [(i, i ^ 1) for i in range(16)]
LIMIT = 20


def place(branches, default):
    for hit, value in branches:
        default = jnp.where(hit, value, default)
    return default


LANDS = (3, 7, 3, 7)
STEPS = (3, 2, 7, 1, 6, 5, 4)


def column_of(group, pos):
    return group // 2 * 16 + (group % 2 * 8 + pos - 3) % 16


def spread(parts, x_at, z_at):
    share = parts[0].shape[0] // 8
    turned = (z_at + 3) % 16
    group, pos = x_at * 2 + turned // 8, turned % 8
    landing = [[(LANDS[m] + h) % 8 for h in (0, 1)] for m in range(4)]
    sent = []
    for m in (3, 2, 1):
        block = lax.ppermute(parts[m], COL, [(h, column_of(m, landing[m][h])) for h in (0, 1)])
        sent.append((group == m, block))
    held = place(sent, parts[0])
    got = {}
    for d in STEPS:
        piece = lax.dynamic_slice_in_dim(held, (pos + d) % 8 * share, share, 0)
        pairs = [(column_of(m, at), column_of(m, (at + d) % 8)) for m in range(4) for at in landing[m]]
        got[d] = lax.ppermute(piece, COL, pairs)
    own = lax.dynamic_slice_in_dim(held, pos * share, share, 0)
    apart = (pos - jnp.where(group % 2 == 0, LANDS[0], LANDS[1])) % 8
    left = place([(apart == d, got[d]) for d in STEPS], own)
    right = place([((apart - 1) % 8 == d, got[d]) for d in STEPS], own)
    return jnp.concatenate([left, right], axis=1)


def update_kernel(
    left_ref, upper_ref, cols_ref, p_ref, q_ref, trailing_ref, out_ref, *rest
):
    parts, (outer_ref, inner_ref, weights_ref, q_held, dense_ref, sems) = rest[:4], rest[4:]
    rank_pad = p_ref.shape[2]
    depth = cols_ref.shape[4]
    copies = []

    def fetch(source, target):
        copies.append(pltpu.make_async_copy(source, target, sems.at[len(copies)]))

    needs = []
    for c in range(4):
        if c % 2 == 0:
            at = slice(2 * c, 2 * c + 4)
            fetch(q_ref.at[:, at], q_held.at[:, at])
        at = slice(4 * c, 4 * c + 4)
        fetch(cols_ref.at[at, :, 1], inner_ref.at[at])
        needs.append(len(copies))
    for c in range(2):
        at = slice(8 * c, 8 * c + 8)
        fetch(cols_ref.at[at, :, 0], outer_ref.at[at])
    fetch(trailing_ref, dense_ref)
    for copy in copies:
        copy.start()
    half = rank_pad // 2
    pair = (2 * rank_pad, 2 * rank_pad)
    t, u = lax.broadcasted_iota(jnp.int32, pair, 0), lax.broadcasted_iota(jnp.int32, pair, 1)
    u_low = u < rank_pad
    u = jnp.where(u_low, u, u - rank_pad)
    late = t >= rank_pad
    t = jnp.where(late, t - rank_pad, t)
    t_low = t < half
    t = jnp.where(t_low, t, t - half) + jnp.where(late, half, 0)
    same = t_low == u_low
    waited = 0
    for zz in range(8):
        while waited < needs[zz // 2]:
            copies[waited].wait()
            waited += 1
        core = lax.dot_general(
            inner_ref[2 * zz : 2 * zz + 2].reshape(2 * rank_pad, depth),
            jnp.concatenate([p_ref[0, zz], p_ref[1, zz]], axis=0),
            (((1,), (1,)), ((), ())),
            preferred_element_type=jnp.float32,
        )
        left_live = t < jnp.where(t_low, left_ref[zz], left_ref[zz + 8])
        upper_live = u < jnp.where(u_low, upper_ref[zz], upper_ref[zz + 8])
        core = jnp.where(same & left_live & upper_live, core, 0.0).astype(BF)
        at = 2 * zz * rank_pad
        weights_ref[at : at + 2 * rank_pad, :] = jnp.dot(
            core, jnp.concatenate([q_held[0, zz], q_held[1, zz]], axis=0), preferred_element_type=jnp.float32
        ).astype(BF)
    for copy in copies[waited:]:
        copy.wait()
    outer = outer_ref[...].reshape(NT * rank_pad, depth)
    product = lax.dot_general(outer, weights_ref[...], (((0,), (0,)), ((), ())), preferred_element_type=jnp.float32)
    done = (dense_ref[...].astype(jnp.float32) - product).astype(BF)
    out_ref[...] = done
    share = done.shape[0] // 32
    for m, part_ref in enumerate(parts):
        for pos in range(8):
            at = column_of(m, pos) * share
            part_ref[pos * share : (pos + 1) * share, :] = done[at : at + share]


def update(left, upper, cols, p_rows, q_rows, trailing):
    height, width = trailing.shape
    rank_pad, depth, half = p_rows.shape[2], cols.shape[4], cols.shape[3]
    vmem, smem = pl.BlockSpec(memory_space=pltpu.VMEM), pl.BlockSpec(memory_space=pltpu.SMEM)
    hbm = pl.BlockSpec(memory_space=pltpu.HBM)
    held = pltpu.VMEM((NT, 2, half, depth), BF)
    return pl.pallas_call(
        update_kernel,
        out_shape=[jax.ShapeDtypeStruct((height, width), BF)] + [jax.ShapeDtypeStruct((height // 4, width), BF)] * 4,
        in_specs=[smem, smem, hbm, vmem, hbm, hbm],
        out_specs=[vmem] * 5,
        scratch_shapes=[held, held, pltpu.VMEM((NT * rank_pad, width), BF), pltpu.VMEM(q_rows.shape, BF), pltpu.VMEM(trailing.shape, BF), pltpu.SemaphoreType.DMA((9,))],
        compiler_params=pltpu.CompilerParams(vmem_limit_bytes=LIMIT << 20),
    )(
        left,
        upper,
        pltpu.with_memory_space_constraint(cols, pltpu.HBM),
        p_rows,
        pltpu.with_memory_space_constraint(q_rows, pltpu.HBM),
        pltpu.with_memory_space_constraint(trailing, pltpu.HBM),
    )


def body(trailing, left_outer, left_inner, upper_outer, upper_inner, left_ranks, upper_ranks):
    core_at = lax.axis_index("core")
    row_at = lax.axis_index("chip") * 2 + core_at
    x_at, z_at = lax.axis_index("xhi"), lax.axis_index("z")
    col_at = x_at * 16 + z_at
    half, depth = left_outer.shape

    both = jnp.concatenate([left_outer, left_inner], axis=0)
    both = lax.all_gather(both, "xhi", axis=0, tiled=True)
    partner = lax.ppermute(upper_outer, "z", SWAP_Z)
    cols = lax.all_gather(both, "z", axis=0, tiled=True)
    cols = cols.reshape(NT, 2, 2, half, -1)

    even = z_at % 2 == 0
    rows = jnp.concatenate(
        [jnp.where(even, upper_outer, partner), jnp.where(even, partner, upper_outer), upper_inner], axis=1
    )
    rows = lax.all_to_all(jnp.broadcast_to(rows[None], (NT // 2,) + rows.shape), "chip", 0, 0)
    across = lax.ppermute(rows, "core", [(0, 1), (1, 0)])
    lower = core_at == 0

    def whole(own, far):
        both = jnp.stack([jnp.where(lower, own, far), jnp.where(lower, far, own)], axis=1)
        return both.reshape((2, 8) + own.shape[1:])

    p_rows = whole(rows[..., :depth], across[..., :depth])
    q_rows = whole(rows[..., depth:], across[..., depth:])

    left = lax.dynamic_index_in_dim(left_ranks, row_at, 0, keepdims=False)
    upper = lax.dynamic_index_in_dim(upper_ranks, col_at // 2, 1, keepdims=False)
    updated, *parts = update(left, upper, cols, p_rows, q_rows, trailing)
    return updated, spread(parts, x_at, z_at)


def solution(mesh):
    fine = Mesh(mesh.devices.reshape(8, 2, 2, 16), ("chip", "core", "xhi", "z"))
    grid = P(ROW, COL)
    turned = P(COL, ROW)
    return jax.shard_map(
        body,
        mesh=fine,
        in_specs=(grid, turned, turned, grid, grid, P(), P()),
        out_specs=(grid, P(ROW + COL, None)),
        check_vma=False,
    )
```
